256 devices in a mesh: rows: 64 (over z, x, core), heads: 4 (over y).
Axes of the slice: x: 4, y: 4, z: 8, core: 2. Of those that a mesh axis runs over, the one named last changes fastest.
Arguments:
- sheet: bfloat16 [1024, 256, 768], P('rows'), may hold values from -16 to 16
- w_query: bfloat16 [768, 768], P(None, 'heads'), may hold values from -0.21875 to 0.21875
- w_key: bfloat16 [768, 768], P(None, 'heads'), may hold values from -0.21875 to 0.21875
- w_value: bfloat16 [768, 768], P(None, 'heads'), may hold values from -0.21875 to 0.21875
- cotangent: bfloat16 [1024, 256, 768], P('rows', None, 'heads'), may hold values from -6 to 6
- lengths: int32 [1024], P('rows'), may hold values from 32 to 256
Outputs:
- input_grad: bfloat16 [1024, 256, 768], P('rows', None, 'heads')
- weight_grad: float32 [768, 3, 768], P('rows', None, 'heads')
The draws below stay inside these ranges and needn't reach their ends.
All inputs are finite; a program needn't handle non-finite values.
Results may differ from the reference program's by a relative error of at most 0.013.
Values may be sent and summed in bfloat16 or wider, within the bound.
A program may use at most 128 MiB of HBM per device.

```python
import jax
import jax.numpy as jnp
from jax import lax

D = 768
HEADS = 12
HEAD_DIM = 64
C = 256
ROWS = 1024
N_HEADS = 4


def place_ends(values, rng, smallest, largest):
    spot = [jax.random.randint(jax.random.fold_in(rng, axis), (), 0, length) for axis, length in enumerate(values.shape)]
    main_axis = values.shape.index(max(values.shape))
    neighbour = spot[:main_axis] + [(spot[main_axis] + 1) % values.shape[main_axis]] + spot[main_axis + 1:]
    return values.at[tuple(spot)].set(smallest).at[tuple(neighbour)].set(largest)


def spiked(drawn, own_key, source, target, shards_of, factor):
    def block_of(position):
        return (jnp.arange(drawn.shape[position]) // (drawn.shape[position] // shards_of)).reshape((-1,) + (1,) * (drawn.ndim - 1 - position))

    near = jax.random.permutation(own_key, shards_of)[block_of(target)]
    second = (block_of(target) + shards_of // 2) % shards_of
    return jnp.where((block_of(source) == near) | (block_of(source) == second), factor * drawn, drawn)


def shard_levels(stream_key, shape, pieces, low, top_value):
    def one(axis_at, shards_of):
        heights = jax.random.uniform(jax.random.fold_in(jax.random.fold_in(stream_key, 6), axis_at), (shards_of,), jnp.float32, low / len(pieces), top_value / len(pieces))
        return jnp.repeat(jnp.exp(heights), shape[axis_at] // shards_of).reshape((-1,) + (1,) * (len(shape) - axis_at - 1))

    loudness = one(*pieces[0])
    for cut in pieces[1:]:
        loudness = loudness * one(*cut)
    return loudness


def gaussian(stream_key, shape, spread, most, cuts=(), kind=jnp.bfloat16):
    values = spread * jax.random.normal(stream_key, shape, jnp.float32)
    if cuts:
        values = values * shard_levels(stream_key, shape, cuts, -0.22, 0.18)
    return jnp.clip(values, -most, most).astype(kind)


def heavy_noise(key, extent, scale, limit, cuts, heavy, kind=jnp.bfloat16):
    array = scale * jax.random.normal(key, extent, jnp.float32)
    if cuts:
        array = array * shard_levels(key, extent, cuts, -0.22, 0.18)
    return jnp.clip(spiked(array, jax.random.fold_in(key, 3), *heavy), -limit, limit).astype(kind)


def setup_inputs(seed: int = 0) -> dict:
    key_of = jax.random.split(jax.random.key(seed), 7)
    return {
        "sheet": heavy_noise(key_of[0], (ROWS, C, D), 1.0, 16.0, ((0, 64),), (0, 2, 64, 4.0)),
        "w_query": gaussian(key_of[1], (D, D), D ** -0.5, 0.21875, ((1, 4),)),
        "w_key": gaussian(key_of[2], (D, D), D ** -0.5, 0.21875, ((1, 4),)),
        "w_value": gaussian(key_of[3], (D, D), D ** -0.5, 0.21875, ((1, 4),)),
        "cotangent": gaussian(key_of[4], (ROWS, C, D), 1.0, 6.0, ((0, 64), (2, 4))),
        "lengths": place_ends(jax.random.randint(key_of[5], (ROWS,), C // 8, C + 1), jax.random.fold_in(key_of[5], 1), C // 8, C).astype(jnp.int32),
    }


def reference(sheet, w_query, w_key, w_value, cotangent, lengths):
    rows, cols, width = sheet.shape
    valid = (jnp.arange(cols, dtype=jnp.int32)[None, :] < lengths[:, None]).astype(jnp.float32)
    scale = 1.0 / jnp.sqrt(jnp.float32(HEAD_DIM * ROWS))
    flat = sheet.reshape(rows * cols, width)

    def project(weight):
        value = jnp.dot(flat, weight, preferred_element_type=jnp.float32).reshape(rows, cols, width)
        return (value * valid[..., None]).astype(jnp.bfloat16)
    query = project(w_query)
    key = project(w_key)
    value = project(w_value)
    split = (rows, cols, HEADS, HEAD_DIM)
    q32 = query.reshape(split).astype(jnp.float32)
    k32 = key.reshape(split).astype(jnp.float32)
    v32 = value.reshape(split).astype(jnp.float32)
    g32 = cotangent.reshape(split).astype(jnp.float32)
    logits = jnp.einsum('rihd,rjhd->hij', q32, k32)
    dprob = jnp.einsum('rihd,rjhd->hij', g32, v32)
    probs = jax.nn.softmax(scale * logits, axis=-1)
    probs_b = probs.astype(jnp.bfloat16)
    inner = lax.optimization_barrier(jnp.sum(probs * dprob, axis=-1, keepdims=True))
    dscore = (scale * probs * (dprob - inner)).astype(jnp.bfloat16)
    ds32 = dscore.astype(jnp.float32)
    mask = valid[..., None]
    dquery = (jnp.einsum('hij,rjhd->rihd', ds32, k32).reshape(rows, cols, width) * mask).astype(jnp.bfloat16)
    dkey = (jnp.einsum('hij,rihd->rjhd', ds32, q32).reshape(rows, cols, width) * mask).astype(jnp.bfloat16)
    dvalue = (jnp.einsum('hij,rihd->rjhd', probs_b.astype(jnp.float32), g32).reshape(rows, cols, width) * mask).astype(jnp.bfloat16)
    group = width // N_HEADS
    total = jnp.zeros((rows * cols, width), jnp.float32)
    for index in range(N_HEADS):
        lo = index * group
        grads = jnp.concatenate([dquery[..., lo:lo + group], dkey[..., lo:lo + group], dvalue[..., lo:lo + group]], axis=-1).reshape(rows * cols, 3 * group)
        weights = jnp.concatenate([w_query[:, lo:lo + group], w_key[:, lo:lo + group], w_value[:, lo:lo + group]], axis=1)
        part = lax.dot_general(grads, weights, (((1,), (1,)), ((), ())), preferred_element_type=jnp.float32)
        rounded = lax.optimization_barrier(part.astype(jnp.bfloat16))
        total = total + rounded.astype(jnp.float32)
    input_grad = total.reshape(rows, cols, width).astype(jnp.bfloat16)

    def weight_term(grad):
        return lax.dot_general(flat, grad.reshape(rows * cols, width), (((0,), (0,)), ((), ())), preferred_element_type=jnp.float32)
    weight_grad = jnp.stack([weight_term(dquery), weight_term(dkey), weight_term(dvalue)], axis=1)
    return (input_grad, weight_grad)
```

```python
import functools

import jax
import jax.numpy as jnp
from jax import lax
from jax.experimental import pallas as pl
from jax.experimental.pallas import tpu as pltpu
from jax.sharding import PartitionSpec as P

HEAD_DIM = 64
MESH = pl.DeviceIdType.MESH
NX, NZ, NY = 4, 8, 4
NH = 3
F32 = jnp.float32
BF16 = jnp.bfloat16


def nt(a, b):
    return lax.dot_general(a, b, (((1,), (1,)), ((), ())), preferred_element_type=F32)


def nn(a, b):
    return lax.dot_general(a, b, (((1,), (0,)), ((), ())), preferred_element_type=F32)


def tn(a, b):
    return lax.dot_general(a, b, (((0,), (0,)), ((), ())), preferred_element_type=F32)


def kernel(
    scale,
    sheet_h, wq, wk, wv, cot_h, lens, out_h, wg_out,
    sheet, cot, w_t, w_cat, vm, q_t, k_t, v_t, g_t,
    u, a_recv, a_sum, x_recv, x_sum, z_recv, full, gat, prob, dsc,
    d_t, part, r2, rl, fin, out_v,
    wg_acc, wg_n, wg_b, wa_recv, wx_recv, wx_sum, wz_recv,
    s_sheet, s_cot, s_out,
    sa, ra, sx, rx, sz, rz, sd, rd, sgz, rgz, sgx, rgx, sgc, rgc,
    s2, r2s, sdir, rdir, srl, rrl, swa, rwa, swx, rwx, swz, rwz,
):
    ri = lax.axis_index("rows")
    y = lax.axis_index("heads")
    core = lax.rem(ri, 2)
    x = lax.rem(ri // 2, NX)
    z = ri // (2 * NX)
    other = 1 - core
    partner = {"rows": (z * NX + x) * 2 + other}
    xs = [lax.rem(x + k, NX) for k in range(1, NX)]
    zs = [lax.rem(z + k, NZ) for k in range(1, NZ)]
    xpeer = [{"rows": (z * NX + xk) * 2 + core} for xk in xs]
    zpeer = [{"rows": (zk * NX + x) * 2 + core} for zk in zs]
    up, dn, opp = lax.rem(y + 1, NY), lax.rem(y + 3, NY), lax.rem(y + 2, NY)
    d_up, d_dn = {"heads": up}, {"heads": dn}

    def remote(src, dst, ss, rs, dev):
        return pltpu.make_async_remote_copy(
            src_ref=src, dst_ref=dst, send_sem=ss, recv_sem=rs, device_id=dev, device_id_type=MESH
        )

    for r in range(16):
        pltpu.make_async_copy(sheet_h.at[r], sheet.at[r], s_sheet.at[r]).start()
        pltpu.make_async_copy(cot_h.at[r], cot.at[r], s_cot.at[r]).start()

    barrier = pltpu.get_barrier_semaphore()
    peers = [partner, d_up, d_dn] + xpeer + zpeer
    for dev in peers:
        pl.semaphore_signal(barrier, inc=1, device_id=dev, device_id_type=MESH)

    w_t[0:192] = wq[...].T
    w_t[192:384] = wk[...].T
    w_t[384:576] = wv[...].T
    w_cat[...] = w_t[...].T

    def mask_row(r, _):
        vm[pl.ds(r, 1), :] = (
            lax.broadcasted_iota(jnp.int32, (1, 256), 1) < lens[r]
        ).astype(F32)
        return 0

    for r in range(16):
        mask_row(r, 0)

    def split_rows(ref, r, mat):
        at = pl.multiple_of(r * 64, 64)
        for h in range(NH):
            ref[h, pl.ds(at, 64), :] = mat[h * 64:(h + 1) * 64].astype(BF16)

    def value_row(r, _):
        pltpu.make_async_copy(sheet_h.at[r], sheet.at[r], s_sheet.at[r]).wait()
        pltpu.make_async_copy(cot_h.at[r], cot.at[r], s_cot.at[r]).wait()
        mat = nt(w_t[384:576], sheet[r]) * vm[pl.ds(r, 1), :]
        split_rows(v_t, r, mat)
        split_rows(g_t, r, cot[r].T)
        return 0

    lax.fori_loop(0, 16, value_row, 0)

    def core_copy(t, h):
        return remote(
            u.at[t, other, h], a_recv.at[t, h], sa.at[t, h], ra.at[t, h], partner
        )

    def x_copy(t, k):
        at = pl.multiple_of(xs[k] * 64, 64)
        return remote(
            a_sum.at[t, :, pl.ds(at, 64), :], x_recv.at[t, k], sx.at[t, k], rx.at[t, k], xpeer[k]
        )

    def z_copy(t, k):
        at = pl.multiple_of(zs[k] * 8, 8)
        return remote(
            x_sum.at[t, :, pl.ds(at, 8), :], z_recv.at[t, k], sz.at[t, k], rz.at[t, k], zpeer[k]
        )

    def outer(t, left, right):
        def one(h, _):
            mat = tn(left[h], right[h])
            u[t, 0, h] = mat[:, :128]
            u[t, 1, h] = mat[:, 128:]
            core_copy(t, h).start()
            return 0

        return one

    def add_core(t):
        for h in range(NH):
            core_copy(t, h).wait_recv()
            a_sum[t, h] = u[t, core, h] + a_recv[t, h]
        for k in range(NX - 1):
            x_copy(t, k).start()

    def add_x(t):
        for k in range(NX - 1):
            x_copy(t, k).wait_recv()
        mine = pl.multiple_of(x * 64, 64)
        x_sum[t] = a_sum[t, :, pl.ds(mine, 64), :] + x_recv[t, 0] + x_recv[t, 1] + x_recv[t, 2]
        for k in range(NZ - 1):
            z_copy(t, k).start()

    def add_z(t):
        for k in range(NZ - 1):
            z_copy(t, k).wait_recv()
        mine = pl.multiple_of(z * 8, 8)
        total = x_sum[t, :, pl.ds(mine, 8), :]
        for k in range(NZ - 1):
            total = total + z_recv[t, k]
        full[core, t] = total

    pl.semaphore_wait(barrier, len(peers))
    lax.fori_loop(0, NH, outer(0, g_t, v_t), 0)

    def query_rows(lo, hi):
        def one(r, _):
            mat = nt(w_t[0:384], sheet[r]) * vm[pl.ds(r, 1), :]
            split_rows(q_t, r, mat[:192])
            split_rows(k_t, r, mat[192:])
            return 0

        lax.fori_loop(lo, hi, one, 0)

    query_rows(0, 5)
    add_core(0)
    query_rows(5, 16)
    add_x(0)
    lax.fori_loop(0, NH, outer(1, q_t, k_t), 0)
    add_core(1)
    add_z(0)
    add_x(1)
    add_z(1)

    half_copy = remote(full.at[core], full.at[core], sd.at[0], rd.at[0], partner)
    half_copy.start()
    half_copy.wait_recv()

    dprob = jnp.concatenate([full[0, 0], full[1, 0]], axis=-1)
    logits = jnp.concatenate([full[0, 1], full[1, 1]], axis=-1) * scale
    top = jnp.max(logits, axis=-1, keepdims=True)
    ex = jnp.exp(logits - top)
    probs = ex / jnp.sum(ex, axis=-1, keepdims=True)
    inner = jnp.sum(probs * dprob, axis=-1, keepdims=True)
    dscore = scale * probs * (dprob - inner)
    tile = jnp.concatenate([probs, dscore], axis=1).astype(BF16)
    block = x * NZ + z
    gat[core, block] = jnp.where(core == 0, tile[:, :, :128].astype(F32), tile[:, :, 128:].astype(F32)).astype(BF16)

    gz = [
        remote(gat.at[core, block], gat.at[core, block], sgz.at[k], rgz.at[k], zpeer[k])
        for k in range(NZ - 1)
    ]
    for c in gz:
        c.start()
    for c in gz:
        c.wait_recv()

    def gx_copy(k):
        src = gat.at[core, pl.ds(pl.multiple_of(x * NZ, NZ), NZ)]
        return remote(src, src, sgx.at[k], rgx.at[k], xpeer[k])

    def gc_copy(k):
        owner = lax.rem(x + NX - k, NX)
        src = gat.at[core, pl.ds(pl.multiple_of(owner * NZ, NZ), NZ)]
        return remote(src, src, sgc.at[k], rgc.at[k], partner)

    for k in range(NX - 1):
        gx_copy(k).start()
    gc_copy(0).start()
    for k in range(NX - 1):
        gx_copy(k).wait_recv()
        gc_copy(k + 1).start()
    for k in range(NX):
        gc_copy(k).wait_recv()

    def unpack(h, _):
        for ch in range(2):
            mat = gat[ch, :, h].astype(F32)
            prob[h, :, ch * 128:(ch + 1) * 128] = mat[:, :8].reshape(256, 128).astype(BF16)
            dsc[h, :, ch * 128:(ch + 1) * 128] = mat[:, 8:].reshape(256, 128).astype(BF16)
        return 0

    lax.fori_loop(0, NH, unpack, 0)

    def back(h, _):
        at = pl.multiple_of(h * 64, 64)
        for t in range(3):
            if t == 0:
                mat = nt(k_t[h], dsc[h])
            elif t == 1:
                mat = nn(q_t[h], dsc[h])
            else:
                mat = nn(g_t[h], prob[h])
            for r in range(16):
                piece = (mat[r * 64:(r + 1) * 64] * vm[r:r + 1, :]).astype(BF16)
                lane = (r % 2) * 256
                d_t[r // 2, pl.ds(at + t * 192, 64), lane:lane + 256] = piece
        return 0

    lax.fori_loop(0, NH, back, 0)

    def rows_of(dest, lo, n):
        return pl.ds(pl.multiple_of(dest * 192 + lo, 16), n)

    def hop_up(c):
        return remote(part.at[c, rows_of(opp, 0, 96), :], r2.at[0, c], s2.at[0, c], r2s.at[0, c], d_up)

    def hop_dn(c):
        return remote(part.at[c, rows_of(opp, 96, 96), :], r2.at[1, c], s2.at[1, c], r2s.at[1, c], d_dn)

    def dir_up(c):
        return remote(
            part.at[c, rows_of(up, 96, 96), :], fin.at[0, c, 96:192, :], sdir.at[0, c], rdir.at[0, c], d_up
        )

    def dir_dn(c):
        return remote(
            part.at[c, rows_of(dn, 0, 96), :], fin.at[1, c, 0:96, :], sdir.at[1, c], rdir.at[1, c], d_dn
        )

    def rel_up(c):
        return remote(rl.at[0, c], fin.at[0, c, 0:96, :], srl.at[0, c], rrl.at[0, c], d_up)

    def rel_dn(c):
        return remote(rl.at[1, c], fin.at[1, c, 96:192, :], srl.at[1, c], rrl.at[1, c], d_dn)

    wg_acc[...] = jnp.zeros_like(wg_acc)

    def parts(c, _):
        part[c] = nn(w_cat[...], d_t[c]).astype(BF16)
        hop_up(c).start()
        hop_dn(c).start()
        dir_up(c).start()
        dir_dn(c).start()
        wg_acc[...] += nn(d_t[c], sheet[pl.ds(2 * c, 2)].reshape(512, 768))
        return 0

    lax.fori_loop(0, 8, parts, 0)

    def relay(c, _):
        hop_up(c).wait_recv()
        rl[0, c] = (part[c, rows_of(up, 0, 96), :].astype(F32) + r2[0, c].astype(F32)).astype(BF16)
        rel_up(c).start()
        hop_dn(c).wait_recv()
        rl[1, c] = (part[c, rows_of(dn, 96, 96), :].astype(F32) + r2[1, c].astype(F32)).astype(BF16)
        rel_dn(c).start()
        return 0

    wg_n[0:768] = wg_acc[...].T
    wg_n[768:784] = jnp.zeros((16, 576), F32)
    for g in range(64):
        gc, gx, gz_ = g % 2, (g // 2) % NX, g // (2 * NX)
        wg_b[gc, gx, gz_] = wg_n[12 * g:12 * g + 16, :]

    wa = remote(wg_b.at[other], wa_recv, swa.at[0], rwa.at[0], partner)
    wa.start()
    lax.fori_loop(0, 3, relay, 0)
    wa.wait_recv()
    wa_recv[...] = wa_recv[...] + wg_b[core]

    def wx_copy(k):
        return remote(wa_recv.at[xs[k]], wx_recv.at[k], swx.at[k], rwx.at[k], xpeer[k])

    def wz_copy(k):
        return remote(wx_sum.at[zs[k]], wz_recv.at[k], swz.at[k], rwz.at[k], zpeer[k])

    for k in range(NX - 1):
        wx_copy(k).start()
    lax.fori_loop(3, 6, relay, 0)
    for k in range(NX - 1):
        wx_copy(k).wait_recv()
    wx_sum[...] = wa_recv[x] + wx_recv[0] + wx_recv[1] + wx_recv[2]
    for k in range(NZ - 1):
        wz_copy(k).start()
    lax.fori_loop(6, 8, relay, 0)
    for k in range(NZ - 1):
        wz_copy(k).wait_recv()
    total = wx_sum[z]
    for k in range(NZ - 1):
        total = total + wz_recv[k]
    wg_out[...] = total[:12]

    def out_copy(c):
        return pltpu.make_async_copy(out_v.at[c], out_h.at[c], s_out.at[c])

    def finish(c, _):
        dir_up(c).wait_recv()
        dir_dn(c).wait_recv()
        rel_up(c).wait_recv()
        rel_dn(c).wait_recv()
        tot = part[c, rows_of(y, 0, 192), :].astype(F32) + fin[0, c].astype(F32) + fin[1, c].astype(F32)
        out_v[c] = tot.astype(BF16).T
        out_copy(c).start()
        return 0

    lax.fori_loop(0, 8, finish, 0)

    for t in range(2):
        for h in range(NH):
            core_copy(t, h).wait_send()
        for k in range(NX - 1):
            x_copy(t, k).wait_send()
        for k in range(NZ - 1):
            z_copy(t, k).wait_send()
    half_copy.wait_send()
    for c in gz:
        c.wait_send()
    for k in range(NX - 1):
        gx_copy(k).wait_send()
        wx_copy(k).wait_send()
    for k in range(NX):
        gc_copy(k).wait_send()
    wa.wait_send()
    for k in range(NZ - 1):
        wz_copy(k).wait_send()

    def drain(c, _):
        for cp in (hop_up, hop_dn, dir_up, dir_dn, rel_up, rel_dn):
            cp(c).wait_send()
        out_copy(c).wait()
        return 0

    lax.fori_loop(0, 8, drain, 0)


def body(sheet, w_query, w_key, w_value, cotangent, lengths):
    scale = float((HEAD_DIM * sheet.shape[0] * lax.axis_size("rows")) ** -0.5)
    vmem = pl.BlockSpec(memory_space=pltpu.VMEM)
    anyw = pl.BlockSpec(memory_space=pl.ANY)
    dma = pltpu.SemaphoreType.DMA
    V = pltpu.VMEM
    scratch = [
        V((16, 256, 768), BF16), V((16, 256, 192), BF16), V((576, 768), BF16), V((768, 576), BF16),
        V((16, 256), F32),
        V((3, 1024, 256), BF16), V((3, 1024, 256), BF16), V((3, 1024, 256), BF16), V((3, 1024, 256), BF16),
        V((2, 2, 3, 256, 128), F32), V((2, 3, 256, 128), F32), V((2, 3, 256, 128), F32),
        V((2, 3, 3, 64, 128), F32), V((2, 3, 64, 128), F32),
        V((2, 7, 3, 8, 128), F32), V((2, 2, 3, 8, 128), F32),
        V((2, 32, 3, 16, 128), BF16), V((3, 256, 256), BF16), V((3, 256, 256), BF16),
        V((8, 576, 512), BF16), V((8, 768, 512), BF16), V((2, 8, 96, 512), BF16), V((2, 8, 96, 512), BF16),
        V((2, 8, 192, 512), BF16), V((8, 512, 192), BF16),
        V((576, 768), F32), V((784, 576), F32), V((2, 4, 8, 16, 576), F32), V((4, 8, 16, 576), F32),
        V((3, 8, 16, 576), F32), V((8, 16, 576), F32), V((7, 16, 576), F32),
        dma((16,)), dma((16,)), dma((8,)),
        dma((2, 3)), dma((2, 3)), dma((2, 3)), dma((2, 3)), dma((2, 7)), dma((2, 7)), dma((1,)), dma((1,)),
        dma((7,)), dma((7,)), dma((3,)), dma((3,)), dma((4,)), dma((4,)),
        dma((2, 8)), dma((2, 8)), dma((2, 8)), dma((2, 8)), dma((2, 8)), dma((2, 8)),
        dma((1,)), dma((1,)), dma((3,)), dma((3,)), dma((7,)), dma((7,)),
    ]
    out, wg = pl.pallas_call(
        functools.partial(kernel, scale),
        out_shape=(jax.ShapeDtypeStruct((8, 512, 192), BF16), jax.ShapeDtypeStruct((12, 576), F32)),
        in_specs=[anyw, vmem, vmem, vmem, anyw, pl.BlockSpec(memory_space=pltpu.SMEM)],
        out_specs=(anyw, vmem),
        scratch_shapes=scratch,
        compiler_params=pltpu.CompilerParams(
            collective_id=0, has_side_effects=True, vmem_limit_bytes=63 * 1024 * 1024
        ),
    )(sheet, w_query, w_key, w_value, cotangent, lengths)
    return out.reshape(16, 256, 192), wg.reshape(12, 3, 192)


def solution(mesh):
    in_specs = (
        P("rows", None, None),
        P(None, "heads"),
        P(None, "heads"),
        P(None, "heads"),
        P("rows", None, "heads"),
        P("rows"),
    )
    out_specs = (P("rows", None, "heads"), P("rows", None, "heads"))
    return jax.shard_map(body, mesh=mesh, in_specs=in_specs, out_specs=out_specs, check_vma=False)
```

```python
import functools

import jax
import jax.numpy as jnp
from jax import lax
from jax.experimental import pallas as pl
from jax.experimental.pallas import tpu as pltpu
from jax.sharding import PartitionSpec as P

HEAD_DIM = 64
MESH = pl.DeviceIdType.MESH
NX, NZ, NY = 4, 8, 4
NH = 3
F32 = jnp.float32
BF16 = jnp.bfloat16


def nt(a, b):
    return lax.dot_general(a, b, (((1,), (1,)), ((), ())), preferred_element_type=F32)


def nn(a, b):
    return lax.dot_general(a, b, (((1,), (0,)), ((), ())), preferred_element_type=F32)


def tn(a, b):
    return lax.dot_general(a, b, (((0,), (0,)), ((), ())), preferred_element_type=F32)


def kernel(
    scale,
    sheet_h, wq, wk, wv, cot_h, lens, out_h, wg_out,
    sheet, w_t, w_cat, vm, q_t, k_t, v_t, g_t,
    u, a_recv, a_sum, x_recv, x_sum, z_recv, full, gat, prob, dsc,
    d_t, part, r2, rl, fin, out_v,
    wg_acc, wg_n, wg_b, wa_recv, wx_recv, wx_sum, wz_recv,
    s_sheet, s_cot, s_w, s_out,
    sa, ra, sx, rx, sz, rz, sd, rd, sgz, rgz, sgx, rgx, sgc, rgc,
    s2, r2s, sdir, rdir, srl, rrl, swa, rwa, swx, rwx, swz, rwz,
):
    ri = lax.axis_index("rows")
    y = lax.axis_index("heads")
    core = lax.rem(ri, 2)
    x = lax.rem(ri // 2, NX)
    z = ri // (2 * NX)
    other = 1 - core
    partner = {"rows": (z * NX + x) * 2 + other}
    xs = [lax.rem(x + k, NX) for k in range(1, NX)]
    zs = [lax.rem(z + k, NZ) for k in range(1, NZ)]
    xpeer = [{"rows": (z * NX + xk) * 2 + core} for xk in xs]
    zpeer = [{"rows": (zk * NX + x) * 2 + core} for zk in zs]
    up, dn, opp = lax.rem(y + 1, NY), lax.rem(y + 3, NY), lax.rem(y + 2, NY)
    d_up, d_dn = {"heads": up}, {"heads": dn}

    def remote(src, dst, ss, rs, dev):
        return pltpu.make_async_remote_copy(
            src_ref=src, dst_ref=dst, send_sem=ss, recv_sem=rs, device_id=dev, device_id_type=MESH
        )

    def w_copy(t):
        return pltpu.make_async_copy((wq, wk, wv)[t], w_t.at[192 * t:192 * t + 192], s_w.at[t])

    def sheet_copy(r):
        return pltpu.make_async_copy(sheet_h.at[r], sheet.at[r], s_sheet.at[r])

    def cot_copy(r):
        at = pl.multiple_of(r * 64, 64)
        return pltpu.make_async_copy(cot_h.at[r], g_t.at[:, pl.ds(at, 64), :], s_cot.at[r])

    w_copy(2).start()
    for r in range(16):
        sheet_copy(r).start()
    for r in range(16):
        cot_copy(r).start()
    w_copy(0).start()
    w_copy(1).start()

    barrier = pltpu.get_barrier_semaphore()
    peers = [partner, d_up, d_dn] + xpeer + zpeer
    for dev in peers:
        pl.semaphore_signal(barrier, inc=1, device_id=dev, device_id_type=MESH)

    for r in range(16):
        vm[r:r + 1, :] = (lax.broadcasted_iota(jnp.int32, (1, 256), 1) < lens[r]).astype(F32)

    def split_rows(ref, r, mat):
        at = pl.multiple_of(r * 64, 64)
        for h in range(NH):
            ref[h, pl.ds(at, 64), :] = mat[h * 64:(h + 1) * 64].astype(BF16)

    def value_rows(i, _):
        for n in range(4):
            sheet_copy(4 * i + n).wait()
        mat = nt(w_t[384:576], sheet[pl.ds(4 * i, 4)].reshape(1024, 768))
        for n in range(4):
            split_rows(v_t, 4 * i + n, mat[:, 256 * n:256 * n + 256] * vm[pl.ds(4 * i + n, 1), :])
        return 0

    w_copy(2).wait()
    lax.fori_loop(0, 4, value_rows, 0)

    def core_copy(t, h):
        return remote(
            u.at[t, other, h], a_recv.at[t, h], sa.at[t, h], ra.at[t, h], partner
        )

    def x_copy(t, k):
        at = pl.multiple_of(xs[k] * 64, 64)
        return remote(
            a_sum.at[t, :, pl.ds(at, 64), :], x_recv.at[t, k], sx.at[t, k], rx.at[t, k], xpeer[k]
        )

    def z_copy(t, k):
        at = pl.multiple_of(zs[k] * 8, 8)
        return remote(
            x_sum.at[t, :, pl.ds(at, 8), :], z_recv.at[t, k], sz.at[t, k], rz.at[t, k], zpeer[k]
        )

    def outer(t, left, right):
        def one(h, _):
            mat = tn(left[h], right[h])
            u[t, 0, h] = mat[:, :128]
            u[t, 1, h] = mat[:, 128:]
            core_copy(t, h).start()
            return 0

        return one

    def add_core(t):
        for h in range(NH):
            core_copy(t, h).wait_recv()
            a_sum[t, h] = u[t, core, h] + a_recv[t, h]
        for k in range(NX - 1):
            x_copy(t, k).start()

    def add_x(t):
        for k in range(NX - 1):
            x_copy(t, k).wait_recv()
        mine = pl.multiple_of(x * 64, 64)
        x_sum[t] = a_sum[t, :, pl.ds(mine, 64), :] + x_recv[t, 0] + x_recv[t, 1] + x_recv[t, 2]
        for k in range(NZ - 1):
            z_copy(t, k).start()

    def add_z(t):
        for k in range(NZ - 1):
            z_copy(t, k).wait_recv()
        mine = pl.multiple_of(z * 8, 8)
        total = x_sum[t, :, pl.ds(mine, 8), :]
        for k in range(NZ - 1):
            total = total + z_recv[t, k]
        full[core, t] = total

    for r in range(16):
        cot_copy(r).wait()
    pl.semaphore_wait(barrier, len(peers))
    lax.fori_loop(0, NH, outer(0, g_t, v_t), 0)

    def query_rows(lo, hi):
        def one(i, _):
            mat = nt(w_t[0:384], sheet[pl.ds(4 * i, 4)].reshape(1024, 768))
            for n in range(4):
                sub = mat[:, 256 * n:256 * n + 256] * vm[pl.ds(4 * i + n, 1), :]
                split_rows(q_t, 4 * i + n, sub[:192])
                split_rows(k_t, 4 * i + n, sub[192:])
            return 0

        lax.fori_loop(lo, hi, one, 0)

    w_copy(0).wait()
    w_copy(1).wait()
    query_rows(0, 1)
    add_core(0)
    query_rows(1, 4)
    add_x(0)
    lax.fori_loop(0, NH, outer(1, q_t, k_t), 0)
    add_core(1)
    add_z(0)
    add_x(1)
    add_z(1)

    half_copy = remote(full.at[core], full.at[core], sd.at[0], rd.at[0], partner)
    half_copy.start()
    w_cat[...] = w_t[...].T
    half_copy.wait_recv()

    dprob = jnp.concatenate([full[0, 0], full[1, 0]], axis=-1)
    logits = jnp.concatenate([full[0, 1], full[1, 1]], axis=-1) * scale
    top = jnp.max(logits, axis=-1, keepdims=True)
    ex = jnp.exp(logits - top)
    probs = ex / jnp.sum(ex, axis=-1, keepdims=True)
    inner = jnp.sum(probs * dprob, axis=-1, keepdims=True)
    dscore = scale * probs * (dprob - inner)
    tile = jnp.concatenate([probs, dscore], axis=1).astype(BF16)
    block = x * NZ + z
    gat[core, block] = jnp.where(core == 0, tile[:, :, :128].astype(F32), tile[:, :, 128:].astype(F32)).astype(BF16)

    gz = [
        remote(gat.at[core, block], gat.at[core, block], sgz.at[k], rgz.at[k], zpeer[k])
        for k in range(NZ - 1)
    ]
    for c in gz:
        c.start()
    for c in gz:
        c.wait_recv()

    def gx_copy(k):
        src = gat.at[core, pl.ds(pl.multiple_of(x * NZ, NZ), NZ)]
        return remote(src, src, sgx.at[k], rgx.at[k], xpeer[k])

    def gc_copy(k):
        owner = lax.rem(x + NX - k, NX)
        src = gat.at[core, pl.ds(pl.multiple_of(owner * NZ, NZ), NZ)]
        return remote(src, src, sgc.at[k], rgc.at[k], partner)

    for k in range(NX - 1):
        gx_copy(k).start()
    gc_copy(0).start()
    for k in range(NX - 1):
        gx_copy(k).wait_recv()
        gc_copy(k + 1).start()
    for k in range(NX):
        gc_copy(k).wait_recv()

    def unpack(h, _):
        for ch in range(2):
            mat = gat[ch, :, h].astype(F32)
            prob[h, :, ch * 128:(ch + 1) * 128] = mat[:, :8].reshape(256, 128).astype(BF16)
            dsc[h, :, ch * 128:(ch + 1) * 128] = mat[:, 8:].reshape(256, 128).astype(BF16)
        return 0

    lax.fori_loop(0, NH, unpack, 0)

    def back(h, _):
        at = pl.multiple_of(h * 64, 64)
        for t in range(3):
            if t == 0:
                mat = nt(k_t[h], dsc[h])
            elif t == 1:
                mat = nn(q_t[h], dsc[h])
            else:
                mat = nn(g_t[h], prob[h])
            for r in range(16):
                piece = (mat[r * 64:(r + 1) * 64] * vm[r:r + 1, :]).astype(BF16)
                lane = (r % 2) * 256
                d_t[r // 2, pl.ds(at + t * 192, 64), lane:lane + 256] = piece
        return 0

    lax.fori_loop(0, NH, back, 0)

    def rows_of(dest, lo, n):
        return pl.ds(pl.multiple_of(dest * 192 + lo, 16), n)

    def hop_up(c):
        return remote(part.at[c, rows_of(opp, 0, 96), :], r2.at[0, c], s2.at[0, c], r2s.at[0, c], d_up)

    def hop_dn(c):
        return remote(part.at[c, rows_of(opp, 96, 96), :], r2.at[1, c], s2.at[1, c], r2s.at[1, c], d_dn)

    def dir_up(c):
        return remote(
            part.at[c, rows_of(up, 96, 96), :], fin.at[0, c, 96:192, :], sdir.at[0, c], rdir.at[0, c], d_up
        )

    def dir_dn(c):
        return remote(
            part.at[c, rows_of(dn, 0, 96), :], fin.at[1, c, 0:96, :], sdir.at[1, c], rdir.at[1, c], d_dn
        )

    def rel_up(c):
        return remote(rl.at[0, c], fin.at[0, c, 0:96, :], srl.at[0, c], rrl.at[0, c], d_up)

    def rel_dn(c):
        return remote(rl.at[1, c], fin.at[1, c, 96:192, :], srl.at[1, c], rrl.at[1, c], d_dn)

    wg_acc[...] = jnp.zeros_like(wg_acc)

    def parts(c, _):
        part[c] = nn(w_cat[...], d_t[c]).astype(BF16)
        hop_up(c).start()
        hop_dn(c).start()
        dir_up(c).start()
        dir_dn(c).start()
        wg_acc[...] += nn(d_t[c], sheet[pl.ds(2 * c, 2)].reshape(512, 768))
        return 0

    lax.fori_loop(0, 8, parts, 0)

    def relay(c, _):
        hop_up(c).wait_recv()
        rl[0, c] = (part[c, rows_of(up, 0, 96), :].astype(F32) + r2[0, c].astype(F32)).astype(BF16)
        rel_up(c).start()
        hop_dn(c).wait_recv()
        rl[1, c] = (part[c, rows_of(dn, 96, 96), :].astype(F32) + r2[1, c].astype(F32)).astype(BF16)
        rel_dn(c).start()
        return 0

    wg_n[0:768] = wg_acc[...].T
    wg_n[768:784] = jnp.zeros((16, 576), F32)
    for g in range(64):
        gc, gx, gz_ = g % 2, (g // 2) % NX, g // (2 * NX)
        wg_b[gc, gx, gz_] = wg_n[12 * g:12 * g + 16, :]

    wa = remote(wg_b.at[other], wa_recv, swa.at[0], rwa.at[0], partner)
    wa.start()
    lax.fori_loop(0, 3, relay, 0)
    wa.wait_recv()
    wa_recv[...] = wa_recv[...] + wg_b[core]

    def wx_copy(k):
        return remote(wa_recv.at[xs[k]], wx_recv.at[k], swx.at[k], rwx.at[k], xpeer[k])

    def wz_copy(k):
        return remote(wx_sum.at[zs[k]], wz_recv.at[k], swz.at[k], rwz.at[k], zpeer[k])

    for k in range(NX - 1):
        wx_copy(k).start()
    lax.fori_loop(3, 6, relay, 0)
    for k in range(NX - 1):
        wx_copy(k).wait_recv()
    wx_sum[...] = wa_recv[x] + wx_recv[0] + wx_recv[1] + wx_recv[2]
    for k in range(NZ - 1):
        wz_copy(k).start()
    lax.fori_loop(6, 8, relay, 0)
    for k in range(NZ - 1):
        wz_copy(k).wait_recv()
    total = wx_sum[z]
    for k in range(NZ - 1):
        total = total + wz_recv[k]
    for t in range(3):
        wg_out[:, t, :] = total[:12, 192 * t:192 * t + 192]

    def out_copy(c):
        rows = pl.ds(2 * c, 2)
        return pltpu.make_async_copy(out_v.at[rows], out_h.at[rows], s_out.at[c])

    def finish(c, _):
        dir_up(c).wait_recv()
        dir_dn(c).wait_recv()
        rel_up(c).wait_recv()
        rel_dn(c).wait_recv()
        tot = part[c, rows_of(y, 0, 192), :].astype(F32) + fin[0, c].astype(F32) + fin[1, c].astype(F32)
        out_v[2 * c] = tot[:, :256].astype(BF16)
        out_v[2 * c + 1] = tot[:, 256:].astype(BF16)
        out_copy(c).start()
        return 0

    lax.fori_loop(0, 8, finish, 0)

    for t in range(2):
        for h in range(NH):
            core_copy(t, h).wait_send()
        for k in range(NX - 1):
            x_copy(t, k).wait_send()
        for k in range(NZ - 1):
            z_copy(t, k).wait_send()
    half_copy.wait_send()
    for c in gz:
        c.wait_send()
    for k in range(NX - 1):
        gx_copy(k).wait_send()
        wx_copy(k).wait_send()
    for k in range(NX):
        gc_copy(k).wait_send()
    wa.wait_send()
    for k in range(NZ - 1):
        wz_copy(k).wait_send()

    def drain(c, _):
        for cp in (hop_up, hop_dn, dir_up, dir_dn, rel_up, rel_dn):
            cp(c).wait_send()
        out_copy(c).wait()
        return 0

    lax.fori_loop(0, 8, drain, 0)


def body(sheet, w_query, w_key, w_value, cotangent, lengths):
    scale = float((HEAD_DIM * sheet.shape[0] * lax.axis_size("rows")) ** -0.5)
    vmem = pl.BlockSpec(memory_space=pltpu.VMEM)
    anyw = pl.BlockSpec(memory_space=pl.ANY)
    dma = pltpu.SemaphoreType.DMA
    V = pltpu.VMEM
    scratch = [
        V((16, 256, 768), BF16), V((576, 768), BF16), V((768, 576), BF16),
        V((16, 256), F32),
        V((3, 1024, 256), BF16), V((3, 1024, 256), BF16), V((3, 1024, 256), BF16), V((3, 1024, 256), BF16),
        V((2, 2, 3, 256, 128), F32), V((2, 3, 256, 128), F32), V((2, 3, 256, 128), F32),
        V((2, 3, 3, 64, 128), F32), V((2, 3, 64, 128), F32),
        V((2, 7, 3, 8, 128), F32), V((2, 2, 3, 8, 128), F32),
        V((2, 32, 3, 16, 128), BF16), V((3, 256, 256), BF16), V((3, 256, 256), BF16),
        V((8, 576, 512), BF16), V((8, 768, 512), BF16), V((2, 8, 96, 512), BF16), V((2, 8, 96, 512), BF16),
        V((2, 8, 192, 512), BF16), V((16, 192, 256), BF16),
        V((576, 768), F32), V((784, 576), F32), V((2, 4, 8, 16, 576), F32), V((4, 8, 16, 576), F32),
        V((3, 8, 16, 576), F32), V((8, 16, 576), F32), V((7, 16, 576), F32),
        dma((16,)), dma((16,)), dma((3,)), dma((8,)),
        dma((2, 3)), dma((2, 3)), dma((2, 3)), dma((2, 3)), dma((2, 7)), dma((2, 7)), dma((1,)), dma((1,)),
        dma((7,)), dma((7,)), dma((3,)), dma((3,)), dma((4,)), dma((4,)),
        dma((2, 8)), dma((2, 8)), dma((2, 8)), dma((2, 8)), dma((2, 8)), dma((2, 8)),
        dma((1,)), dma((1,)), dma((3,)), dma((3,)), dma((7,)), dma((7,)),
    ]
    out, wg = pl.pallas_call(
        functools.partial(kernel, scale),
        out_shape=(jax.ShapeDtypeStruct((16, 192, 256), BF16), jax.ShapeDtypeStruct((12, 3, 192), F32)),
        in_specs=[anyw] * 5 + [pl.BlockSpec(memory_space=pltpu.SMEM)],
        out_specs=(anyw, vmem),
        scratch_shapes=scratch,
        compiler_params=pltpu.CompilerParams(
            collective_id=0, has_side_effects=True, vmem_limit_bytes=56 * 1024 * 1024
        ),
    )(
        sheet, w_query.T, w_key.T, w_value.T,
        cotangent.transpose(0, 2, 1).reshape(16, NH, HEAD_DIM, 256), lengths,
    )
    return out.transpose(0, 2, 1), wg


def solution(mesh):
    in_specs = (
        P("rows", None, None),
        P(None, "heads"),
        P(None, "heads"),
        P(None, "heads"),
        P("rows", None, "heads"),
        P("rows"),
    )
    out_specs = (P("rows", None, "heads"), P("rows", None, "heads"))
    return jax.shard_map(body, mesh=mesh, in_specs=in_specs, out_specs=out_specs, check_vma=False)
```

```python
import functools

import jax
import jax.numpy as jnp
from jax import lax
from jax.experimental import pallas as pl
from jax.experimental.pallas import tpu as pltpu
from jax.sharding import PartitionSpec as P

HEAD_DIM = 64
MESH = pl.DeviceIdType.MESH
NX, NZ, NY = 4, 8, 4
NH = 3
F32 = jnp.float32
BF16 = jnp.bfloat16


def nt(a, b):
    return lax.dot_general(a, b, (((1,), (1,)), ((), ())), preferred_element_type=F32)


def nn(a, b):
    return lax.dot_general(a, b, (((1,), (0,)), ((), ())), preferred_element_type=F32)


def tn(a, b):
    return lax.dot_general(a, b, (((0,), (0,)), ((), ())), preferred_element_type=F32)


def kernel(
    scale,
    sheet_h, wq, wk, wv, cot_h, lens, out_h, wg_out,
    sheet, w_t, w_c, w_vc, vm, q_t, k_t, v_t, g_t,
    w_far, wv_far, w_out, q_far, k_far, g_far,
    u, a_recv, a_sum, x_recv, x_sum, z_recv, full, gat, gat_far, prob, dsc,
    acc, out_v, wg_acc, wg_n, wg_b, wa_recv, wx_recv, wx_sum, wz_recv,
    s_sheet, s_cot, s_w, s_out,
    sa, ra, sx, rx, sz, rz, sd, rd, sgz, rgz, sgx, rgx, sgc, rgc,
    swy, rwy, sww, rww, swc, rwc, sg, rg, sgr, rgr, sty, rty, soz, roz, sox, rox, soc, roc,
    swa, rwa, swx, rwx, swz, rwz,
):
    ri = lax.axis_index("rows")
    y = lax.axis_index("heads")
    core = lax.rem(ri, 2)
    x = lax.rem(ri // 2, NX)
    z = ri // (2 * NX)
    other = 1 - core
    block = x * NZ + z
    partner = {"rows": (z * NX + x) * 2 + other}
    xs = [lax.rem(x + k, NX) for k in range(1, NX)]
    zs = [lax.rem(z + k, NZ) for k in range(1, NZ)]
    ys = [lax.rem(y + k, NY) for k in range(1, NY)]
    xpeer = [{"rows": (z * NX + xk) * 2 + core} for xk in xs]
    zpeer = [{"rows": (zk * NX + x) * 2 + core} for zk in zs]
    ypeer = [{"heads": yk} for yk in ys]
    d_up, d_dn = ypeer[0], ypeer[2]

    def remote(src, dst, ss, rs, dev):
        return pltpu.make_async_remote_copy(
            src_ref=src, dst_ref=dst, send_sem=ss, recv_sem=rs, device_id=dev, device_id_type=MESH
        )

    sends = []

    def send(copies):
        for c in copies:
            c.start()
        sends.extend(copies)

    def receive(copies):
        for c in copies:
            c.wait_recv()

    def w_copy(t):
        return pltpu.make_async_copy((wq, wk, wv)[t], w_t.at[192 * t:192 * t + 192], s_w.at[t])

    def sheet_copy(r):
        return pltpu.make_async_copy(sheet_h.at[r], sheet.at[r], s_sheet.at[r])

    def cot_copy(r):
        at = pl.multiple_of(r * 64, 64)
        return pltpu.make_async_copy(cot_h.at[r], g_t.at[:, pl.ds(at, 64), :], s_cot.at[r])

    w_copy(2).start()
    for r in range(16):
        sheet_copy(r).start()
    w_copy(0).start()
    w_copy(1).start()
    for r in range(16):
        cot_copy(r).start()

    barrier = pltpu.get_barrier_semaphore()
    peers = [partner] + ypeer + xpeer + zpeer
    for dev in peers:
        pl.semaphore_signal(barrier, inc=1, device_id=dev, device_id_type=MESH)

    for r in range(16):
        vm[r:r + 1, :] = (lax.broadcasted_iota(jnp.int32, (1, 256), 1) < lens[r]).astype(F32)

    def split_rows(ref, r, mat):
        at = pl.multiple_of(r * 64, 64)
        for h in range(NH):
            ref[h, pl.ds(at, 64), :] = mat[h * 64:(h + 1) * 64].astype(BF16)

    def value_rows(i, _):
        for n in range(4):
            sheet_copy(4 * i + n).wait()
        mat = nt(w_t[384:576], sheet[pl.ds(4 * i, 4)].reshape(1024, 768))
        for n in range(4):
            split_rows(v_t, 4 * i + n, mat[:, 256 * n:256 * n + 256] * vm[pl.ds(4 * i + n, 1), :])
        return 0

    w_copy(2).wait()
    w_vc[...] = w_t[384:576].T
    lax.fori_loop(0, 4, value_rows, 0)
    for r in range(16):
        cot_copy(r).wait()
    w_copy(0).wait()
    w_copy(1).wait()

    def wy_copies():
        got = []
        for k in range(NY - 1):
            src = w_t.at[pl.ds(pl.multiple_of(core * 192 + x * 48, 16), 48), :]
            got.append(remote(src, w_far.at[k, core, x], swy.at[0, k], rwy.at[0, k], ypeer[k]))
            src = w_vc.at[pl.ds(pl.multiple_of(ys[k] * 192 + x * 48, 16), 48), :]
            got.append(remote(src, wv_far.at[k, x], swy.at[1, k], rwy.at[1, k], ypeer[k]))
        return got

    def wx_copies():
        got = []
        for k in range(NX - 1):
            ref = w_far.at[:, core, x]
            got.append(remote(ref, ref, sww.at[0, k], rww.at[0, k], xpeer[k]))
            ref = wv_far.at[:, x]
            got.append(remote(ref, ref, sww.at[1, k], rww.at[1, k], xpeer[k]))
        return got

    def near_copies(c):
        src = g_t.at[:, 128 * c:128 * c + 128, :]
        return [
            remote(src, g_far.at[0, :, 128 * c:128 * c + 128, :], sg.at[0, c], rg.at[0, c], d_up),
            remote(src, g_far.at[2, :, 128 * c:128 * c + 128, :], sg.at[1, c], rg.at[1, c], d_dn),
        ]

    def relay_copies(c):
        lo, hi = 128 * c, 128 * c + 64
        return [
            remote(
                g_far.at[0, :, lo:lo + 64, :], g_far.at[1, :, lo:lo + 64, :], sgr.at[0, c], rgr.at[0, c], d_up
            ),
            remote(
                g_far.at[2, :, hi:hi + 64, :], g_far.at[1, :, hi:hi + 64, :], sgr.at[1, c], rgr.at[1, c], d_dn
            ),
        ]

    def near(chunks):
        for c in chunks:
            for cp in near_copies(c):
                cp.start()

    def relay(chunks):
        for c in chunks:
            for got, cp in zip(near_copies(c), relay_copies(c)):
                got.wait_recv()
                cp.start()

    def core_copy(t, h):
        return remote(
            u.at[t, other, h], a_recv.at[t, h], sa.at[t, h], ra.at[t, h], partner
        )

    def x_copy(t, k):
        at = pl.multiple_of(xs[k] * 64, 64)
        return remote(
            a_sum.at[t, :, pl.ds(at, 64), :], x_recv.at[t, k], sx.at[t, k], rx.at[t, k], xpeer[k]
        )

    def z_copy(t, k):
        at = pl.multiple_of(zs[k] * 8, 8)
        return remote(
            x_sum.at[t, :, pl.ds(at, 8), :], z_recv.at[t, k], sz.at[t, k], rz.at[t, k], zpeer[k]
        )

    def outer(t, left, right):
        def one(h, _):
            mat = tn(left[h], right[h])
            u[t, 0, h] = mat[:, :128]
            u[t, 1, h] = mat[:, 128:]
            core_copy(t, h).start()
            return 0

        lax.fori_loop(0, NH, one, 0)
        sends.extend(core_copy(t, h) for h in range(NH))

    def add_core(t):
        for h in range(NH):
            core_copy(t, h).wait_recv()
            a_sum[t, h] = u[t, core, h] + a_recv[t, h]
        send([x_copy(t, k) for k in range(NX - 1)])

    def add_x(t):
        receive([x_copy(t, k) for k in range(NX - 1)])
        mine = pl.multiple_of(x * 64, 64)
        x_sum[t] = a_sum[t, :, pl.ds(mine, 64), :] + x_recv[t, 0] + x_recv[t, 1] + x_recv[t, 2]
        send([z_copy(t, k) for k in range(NZ - 1)])

    def add_z(t):
        receive([z_copy(t, k) for k in range(NZ - 1)])
        mine = pl.multiple_of(z * 8, 8)
        total = x_sum[t, :, pl.ds(mine, 8), :]
        for k in range(NZ - 1):
            total = total + z_recv[t, k]
        full[core, t] = total

    def query_rows(qr, kr, weights, lo, hi):
        def one(i, _):
            mat = nt(weights(), sheet[pl.ds(4 * i, 4)].reshape(1024, 768))
            for n in range(4):
                sub = mat[:, 256 * n:256 * n + 256] * vm[pl.ds(4 * i + n, 1), :]
                split_rows(qr, 4 * i + n, sub[:192])
                split_rows(kr, 4 * i + n, sub[192:])
            return 0

        lax.fori_loop(lo, hi, one, 0)

    def own_weights():
        return w_t[0:384]

    pl.semaphore_wait(barrier, len(peers))
    send(wy_copies())
    near([0, 1, 2])
    outer(0, g_t, v_t)
    query_rows(q_t, k_t, own_weights, 0, 1)
    add_core(0)
    query_rows(q_t, k_t, own_weights, 1, 4)
    outer(1, q_t, k_t)
    near([3, 4])
    add_core(1)
    receive(wy_copies())
    send(wx_copies())
    add_x(0)
    rows_y = pl.ds(pl.multiple_of(y * 192, 16), 192)
    w_c[...] = w_t[0:384].T
    w_out[0, :, 0:384] = w_c[rows_y, :]
    w_out[0, :, 384:576] = w_vc[rows_y, :]
    relay([0])
    add_x(1)
    add_z(0)
    add_z(1)

    half_copy = remote(full.at[core], full.at[core], sd.at[0], rd.at[0], partner)
    send([half_copy])
    half_copy.wait_recv()

    dprob = jnp.concatenate([full[0, 0], full[1, 0]], axis=-1)
    logits = jnp.concatenate([full[0, 1], full[1, 1]], axis=-1) * scale
    top = jnp.max(logits, axis=-1, keepdims=True)
    ex = jnp.exp(logits - top)
    probs = ex / jnp.sum(ex, axis=-1, keepdims=True)
    inner = jnp.sum(probs * dprob, axis=-1, keepdims=True)
    dscore = scale * probs * (dprob - inner)
    tile = jnp.concatenate([probs, dscore], axis=1)
    gat[core, block] = jnp.where(core == 0, tile[:, :, :128], tile[:, :, 128:]).astype(BF16)

    own = gat.at[core, block]
    gz = [remote(own, own, sgz.at[k], rgz.at[k], zpeer[k]) for k in range(NZ - 1)]
    ty = [
        remote(own, gat_far.at[k, core, block], sty.at[k], rty.at[k], ypeer[k]) for k in range(NY - 1)
    ]
    send(gz)
    send(ty)
    near([5, 6, 7])

    xblock = pl.ds(pl.multiple_of(x * NZ, NZ), NZ)

    def gx_copy(k):
        src = gat.at[core, xblock]
        return remote(src, src, sgx.at[k], rgx.at[k], xpeer[k])

    def from_x(k):
        return pl.ds(pl.multiple_of(lax.rem(x + NX - k, NX) * NZ, NZ), NZ)

    def gc_copy(k):
        src = gat.at[core, from_x(k)]
        return remote(src, src, sgc.at[k], rgc.at[k], partner)

    def oz_copy(k):
        src = gat_far.at[:, core, block]
        return remote(src, src, soz.at[k], roz.at[k], zpeer[k])

    def ox_copy(s, k):
        src = gat_far.at[s, core, xblock]
        return remote(src, src, sox.at[s, k], rox.at[s, k], xpeer[k])

    def oc_copy(s, k):
        src = gat_far.at[s, core, from_x(k)]
        return remote(src, src, soc.at[s, k], roc.at[s, k], partner)

    receive(wx_copies())
    wc_copy = remote(w_far.at[:, core], w_far.at[:, core], swc.at[0], rwc.at[0], partner)
    send([wc_copy])
    receive(gz)
    send([gx_copy(k) for k in range(NX - 1)])
    send([gc_copy(0)])
    receive(ty)
    send([oz_copy(k) for k in range(NZ - 1)])
    wc_copy.wait_recv()

    def far_weights(s):
        w_c[...] = w_far[s].reshape(384, 768).T
        w_out[s + 1, :, 0:384] = w_c[rows_y, :]
        w_out[s + 1, :, 384:576] = wv_far[s].reshape(192, 192)

    def far_rows(s):
        query_rows(q_far.at[s], k_far.at[s], lambda: w_far[s].reshape(384, 768), 0, 4)

    far_weights(0)
    far_rows(0)
    relay([1, 2])
    for k in range(NX - 1):
        gx_copy(k).wait_recv()
        send([gc_copy(k + 1)])
    receive([oz_copy(k) for k in range(NZ - 1)])
    send([ox_copy(s, k) for s in range(NY - 1) for k in range(NX - 1)])
    send([oc_copy(s, 0) for s in range(NY - 1)])
    receive([gc_copy(k) for k in range(NX)])

    def unpack(src):
        def one(h, _):
            for ch in range(2):
                mat = src(ch, h).astype(F32)
                prob[h, :, ch * 128:(ch + 1) * 128] = mat[:, :8].reshape(256, 128).astype(BF16)
                dsc[h, :, ch * 128:(ch + 1) * 128] = mat[:, 8:].reshape(256, 128).astype(BF16)
            return 0

        lax.fori_loop(0, NH, one, 0)

    def masked(ref, h, mat):
        for r in range(16):
            ref[h, r * 64:(r + 1) * 64, :] = (mat[r * 64:(r + 1) * 64] * vm[r:r + 1, :]).astype(BF16)

    def back_qk(qr, kr):
        def one(h, _):
            dq = nt(kr[h], dsc[h])
            dk = nn(qr[h], dsc[h])
            masked(qr, h, dq)
            masked(kr, h, dk)
            return 0

        lax.fori_loop(0, NH, one, 0)

    def gathered(refs, c):
        cols = []
        for n in range(4):
            at = pl.multiple_of(c * 256 + n * 64, 64)
            cols.append(jnp.concatenate([ref[h, pl.ds(at, 64), :] for ref in refs for h in range(NH)], axis=0))
        return jnp.concatenate(cols, axis=1)

    unpack(lambda ch, h: gat[ch, :, h])
    back_qk(q_t, k_t)

    def back_v(h, _):
        masked(v_t, h, nn(g_t[h], prob[h]))
        return 0

    lax.fori_loop(0, NH, back_v, 0)
    relay([3])
    wg_acc[...] = jnp.zeros_like(wg_acc)

    def own_chunk(c, _):
        grads = gathered((q_t, k_t, v_t), c)
        acc[c] = nn(w_out[0], grads)
        wg_acc[...] += nn(grads, sheet[pl.ds(4 * c, 4)].reshape(1024, 768))
        return 0

    lax.fori_loop(0, 4, own_chunk, 0)
    wg_n[0:768] = wg_acc[...].T
    wg_n[768:784] = jnp.zeros((16, 576), F32)
    for g in range(64):
        gc, gx, gz_ = g % 2, (g // 2) % NX, g // (2 * NX)
        wg_b[gc, gx, gz_] = wg_n[12 * g:12 * g + 16, :].astype(BF16)
    wa = remote(wg_b.at[other], wa_recv, swa.at[0], rwa.at[0], partner)
    send([wa])
    relay([4, 5])

    def far_ready(s):
        for k in range(NX - 1):
            ox_copy(s, k).wait_recv()
            send([oc_copy(s, k + 1)])

    def wx_copy(k):
        return remote(wa_recv.at[xs[k]], wx_recv.at[k], swx.at[k], rwx.at[k], xpeer[k])

    def wz_copy(k):
        return remote(wx_sum.at[zs[k]], wz_recv.at[k], swz.at[k], rwz.at[k], zpeer[k])

    def far_qk(s):
        receive([oc_copy(s, k) for k in range(NX)])
        unpack(lambda ch, h: gat_far[s, ch, :, h])
        back_qk(q_far.at[s], k_far.at[s])

    def far_qk_out(s):
        def one(c, _):
            acc[c] += nn(w_out[s + 1, :, 0:384], gathered((q_far.at[s], k_far.at[s]), c))
            return 0

        lax.fori_loop(0, 4, one, 0)

    def far_v(s, h, c):
        at = pl.multiple_of(c * 256, 256)
        mat = nn(g_far[s, h, pl.ds(at, 256), :], prob[h])
        return [
            (mat[n * 64:(n + 1) * 64] * vm[pl.ds(4 * c + n, 1), :]).astype(BF16) for n in range(4)
        ]

    def far_v_mat(s, c):
        parts = [far_v(s, h, c) for h in range(NH)]
        return jnp.concatenate(
            [jnp.concatenate([parts[h][n] for h in range(NH)], axis=0) for n in range(4)], axis=1
        )

    def far_v_out(s):
        def one(c, _):
            acc[c] += nn(w_out[s + 1, :, 384:576], far_v_mat(s, c))
            return 0

        lax.fori_loop(0, 4, one, 0)

    far_weights(1)
    far_rows(1)
    far_ready(0)
    far_qk(0)
    relay([6, 7])
    far_qk_out(0)
    far_v_out(0)

    wa.wait_recv()
    wa_recv[...] = (wa_recv[...].astype(F32) + wg_b[core].astype(F32)).astype(BF16)
    send([wx_copy(k) for k in range(NX - 1)])

    far_weights(2)
    far_rows(2)
    far_ready(2)
    far_qk(2)
    far_qk_out(2)
    far_v_out(2)

    receive([wx_copy(k) for k in range(NX - 1)])
    wx_sum[...] = (
        wa_recv[x].astype(F32) + wx_recv[0].astype(F32) + wx_recv[1].astype(F32) + wx_recv[2].astype(F32)
    ).astype(BF16)
    send([wz_copy(k) for k in range(NZ - 1)])

    far_ready(1)
    far_qk(1)
    far_qk_out(1)

    def out_copy(c):
        rows = pl.ds(4 * c, 4)
        return pltpu.make_async_copy(out_v.at[rows], out_h.at[rows], s_out.at[c])

    for c in range(4):
        for cc in (2 * c, 2 * c + 1):
            receive(relay_copies(cc))
        tot = acc[c] + nn(w_out[2, :, 384:576], far_v_mat(1, c))
        for n in range(4):
            out_v[4 * c + n] = tot[:, 256 * n:256 * n + 256].astype(BF16)
        out_copy(c).start()

    receive([wz_copy(k) for k in range(NZ - 1)])
    total = wx_sum[z].astype(F32)
    for k in range(NZ - 1):
        total = total + wz_recv[k].astype(F32)
    for t in range(3):
        wg_out[:, t, :] = total[:12, 192 * t:192 * t + 192]

    for c in range(8):
        for cp in near_copies(c) + relay_copies(c):
            cp.wait_send()
    for cp in sends:
        cp.wait_send()
    for c in range(4):
        out_copy(c).wait()


def body(sheet, w_query, w_key, w_value, cotangent, lengths):
    scale = float((HEAD_DIM * sheet.shape[0] * lax.axis_size("rows")) ** -0.5)
    vmem = pl.BlockSpec(memory_space=pltpu.VMEM)
    anyw = pl.BlockSpec(memory_space=pl.ANY)
    dma = pltpu.SemaphoreType.DMA
    V = pltpu.VMEM
    rows = (3, 1024, 256)
    scratch = [
        V((16, 256, 768), BF16), V((576, 768), BF16), V((768, 384), BF16), V((768, 192), BF16), V((16, 256), F32),
        V(rows, BF16), V(rows, BF16), V(rows, BF16), V(rows, BF16),
        V((3, 2, 4, 48, 768), BF16), V((3, 4, 48, 192), BF16), V((4, 192, 576), BF16),
        V((3,) + rows, BF16), V((3,) + rows, BF16), V((3,) + rows, BF16),
        V((2, 2, 3, 256, 128), F32), V((2, 3, 256, 128), F32), V((2, 3, 256, 128), F32),
        V((2, 3, 3, 64, 128), F32), V((2, 3, 64, 128), F32),
        V((2, 7, 3, 8, 128), F32), V((2, 2, 3, 8, 128), F32),
        V((2, 32, 3, 16, 128), BF16), V((3, 2, 32, 3, 16, 128), BF16),
        V((3, 256, 256), BF16), V((3, 256, 256), BF16),
        V((4, 192, 1024), F32), V((16, 192, 256), BF16),
        V((576, 768), F32), V((784, 576), F32), V((2, 4, 8, 16, 576), BF16), V((4, 8, 16, 576), BF16),
        V((3, 8, 16, 576), BF16), V((8, 16, 576), BF16), V((7, 16, 576), BF16),
        dma((16,)), dma((16,)), dma((3,)), dma((4,)),
    ]
    shapes = [
        (2, 3), (2, 3), (2, 7), (1,), (7,), (3,), (4,),
        (2, 3), (2, 3), (1,), (2, 8), (2, 8), (3,), (7,), (3, 3), (3, 4),
        (1,), (3,), (7,),
    ]
    for shape in shapes:
        scratch += [dma(shape), dma(shape)]
    out, wg = pl.pallas_call(
        functools.partial(kernel, scale),
        out_shape=(jax.ShapeDtypeStruct((16, 192, 256), BF16), jax.ShapeDtypeStruct((12, 3, 192), F32)),
        in_specs=[anyw] * 5 + [pl.BlockSpec(memory_space=pltpu.SMEM)],
        out_specs=(anyw, vmem),
        scratch_shapes=scratch,
        compiler_params=pltpu.CompilerParams(
            collective_id=0, has_side_effects=True, vmem_limit_bytes=62 * 1024 * 1024
        ),
    )(
        sheet, w_query.T, w_key.T, w_value.T,
        cotangent.transpose(0, 2, 1).reshape(16, NH, HEAD_DIM, 256), lengths,
    )
    return out.transpose(0, 2, 1), wg


def solution(mesh):
    in_specs = (
        P("rows", None, None),
        P(None, "heads"),
        P(None, "heads"),
        P(None, "heads"),
        P("rows", None, "heads"),
        P("rows"),
    )
    out_specs = (P("rows", None, "heads"), P("rows", None, "heads"))
    return jax.shard_map(body, mesh=mesh, in_specs=in_specs, out_specs=out_specs, check_vma=False)
```

```python
import functools

import jax
import jax.numpy as jnp
from jax import lax
from jax.experimental import pallas as pl
from jax.experimental.pallas import tpu as pltpu
from jax.sharding import PartitionSpec as P

HEAD_DIM = 64
MESH = pl.DeviceIdType.MESH
NX, NZ, NY = 4, 8, 4
NH = 3
F32 = jnp.float32
BF16 = jnp.bfloat16


def nt(a, b):
    return lax.dot_general(a, b, (((1,), (1,)), ((), ())), preferred_element_type=F32)


def nn(a, b):
    return lax.dot_general(a, b, (((1,), (0,)), ((), ())), preferred_element_type=F32)


def tn(a, b):
    return lax.dot_general(a, b, (((0,), (0,)), ((), ())), preferred_element_type=F32)


def kernel(
    scale,
    sheet_h, wq, wk, wv, cot_h, lens, out_h, wg_out,
    sheet, w_t, w_c, w_vc, vm, q_t, k_t, v_t, g_t,
    w_far, wv_far, w_out, q_far, k_far, g_far,
    u, a_recv, a_sum, x_recv, x_sum, z_recv, full, gat, gat_far, prob, dsc,
    acc, out_v, wg_acc, wg_n, wg_b, wa_recv, wz_recv, wx_f, wx_sum, wx_recv,
    s_sheet, s_cot, s_w, s_out,
    sa, ra, sx, rx, sz, rz, sd, rd, sgz, rgz, sgx, rgx, sgc, rgc,
    swy, rwy, sww, rww, swc, rwc, sg, rg, sgr, rgr, sty, rty, soz, roz, sox, rox, soc, roc,
    swa, rwa, swx, rwx, swz, rwz,
):
    ri = lax.axis_index("rows")
    y = lax.axis_index("heads")
    core = lax.rem(ri, 2)
    x = lax.rem(ri // 2, NX)
    z = ri // (2 * NX)
    other = 1 - core
    block = x * NZ + z
    partner = {"rows": (z * NX + x) * 2 + other}
    xs = [lax.rem(x + k, NX) for k in range(1, NX)]
    zs = [lax.rem(z + k, NZ) for k in range(1, NZ)]
    ys = [lax.rem(y + k, NY) for k in range(1, NY)]
    xpeer = [{"rows": (z * NX + xk) * 2 + core} for xk in xs]
    zpeer = [{"rows": (zk * NX + x) * 2 + core} for zk in zs]
    ypeer = [{"heads": yk} for yk in ys]
    d_up, d_dn = ypeer[0], ypeer[2]

    def remote(src, dst, ss, rs, dev):
        return pltpu.make_async_remote_copy(
            src_ref=src, dst_ref=dst, send_sem=ss, recv_sem=rs, device_id=dev, device_id_type=MESH
        )

    sends = []

    def send(copies):
        for c in copies:
            c.start()

    def sent(ref, sem):
        sends.append((ref, sem))

    def flush():
        for ref, sem in sends:
            remote(ref, ref, sem, sem, partner).wait_send()

    def arrived(ref, sem):
        remote(ref, ref, sem, sem, partner).wait_recv()

    def w_copy(t):
        return pltpu.make_async_copy((wq, wk, wv)[t], w_t.at[192 * t:192 * t + 192], s_w.at[0])

    def sheet_copy(i):
        rows = pl.ds(4 * i, 4)
        return pltpu.make_async_copy(sheet_h.at[rows], sheet.at[rows], s_sheet.at[i])

    def cot_copy(r):
        return pltpu.make_async_copy(cot_h.at[r], g_t.at[:, 64 * r:64 * r + 64, :], s_cot.at[0])

    for t in range(3):
        w_copy(t).start()
    for i in range(4):
        sheet_copy(i).start()

    barrier = pltpu.get_barrier_semaphore()
    peers = [partner] + ypeer + xpeer + zpeer
    for dev in peers:
        pl.semaphore_signal(barrier, inc=1, device_id=dev, device_id_type=MESH)

    for r in range(16):
        vm[r:r + 1, :] = (lax.broadcasted_iota(jnp.int32, (1, 256), 1) < lens[r]).astype(F32)

    def split_rows(ref, r, mat):
        at = pl.multiple_of(r * 64, 64)
        for h in range(NH):
            ref[h, pl.ds(at, 64), :] = mat[h * 64:(h + 1) * 64].astype(BF16)

    def value_rows(i, _):
        sheet_copy(i).wait()
        mat = nt(w_t[384:576], sheet[pl.ds(4 * i, 4)].reshape(1024, 768))
        for n in range(4):
            split_rows(v_t, 4 * i + n, mat[:, 256 * n:256 * n + 256] * vm[pl.ds(4 * i + n, 1), :])
        return 0

    pltpu.make_async_copy(w_t, w_t, s_w.at[0]).wait()
    for r in range(16):
        cot_copy(r).start()
    w_vc[...] = w_t[384:576].T
    lax.fori_loop(0, 2, value_rows, 0)
    pl.semaphore_wait(barrier, len(peers))

    quarter = lax.rem(z, 4)
    piece = [quarter, x, x]

    def wy_copies():
        got = []
        for k in range(NY - 1):
            p = piece[k]
            src = w_t.at[pl.ds(pl.multiple_of(core * 192 + p * 48, 16), 48), :]
            got.append(remote(src, w_far.at[k, core, p], swy.at[0], rwy.at[0], ypeer[k]))
            src = w_vc.at[pl.ds(pl.multiple_of(ys[k] * 192 + p * 48, 16), 48), :]
            got.append(remote(src, wv_far.at[k, p], swy.at[1], rwy.at[1], ypeer[k]))
        return got

    hop2 = lax.rem(z + 2 + 4 * lax.rem(z, 2), NZ)
    wpeer = [zpeer[0], zpeer[NZ - 2], {"rows": (hop2 * NX + x) * 2 + core}]

    def wz_copies():
        got = []
        for k in range(3):
            ref = w_far.at[0, core, quarter]
            got.append(remote(ref, ref, sww.at[0], rww.at[0], wpeer[k]))
            ref = wv_far.at[0, quarter]
            got.append(remote(ref, ref, sww.at[1], rww.at[1], wpeer[k]))
        return got

    def wx_copies():
        got = []
        for k in range(3):
            ref = w_far.at[1:3, core, x]
            got.append(remote(ref, ref, sww.at[2], rww.at[2], xpeer[k]))
            ref = wv_far.at[1:3, x]
            got.append(remote(ref, ref, sww.at[3], rww.at[3], xpeer[k]))
        return got

    def near_copies(c):
        src = g_t.at[:, 128 * c:128 * c + 128, :]
        return [
            remote(src, g_far.at[0, :, 128 * c:128 * c + 128, :], sg.at[0], rg.at[0, c], d_up),
            remote(src, g_far.at[2, :, 128 * c:128 * c + 128, :], sg.at[1], rg.at[1, c], d_dn),
        ]

    def relay_copies(c):
        lo, hi = 128 * c, 128 * c + 64
        return [
            remote(
                g_far.at[0, :, lo:lo + 64, :], g_far.at[1, :, lo:lo + 64, :], sgr.at[0], rgr.at[c // 2], d_up
            ),
            remote(
                g_far.at[2, :, hi:hi + 64, :], g_far.at[1, :, hi:hi + 64, :], sgr.at[1], rgr.at[c // 2], d_dn
            ),
        ]

    def near(chunks):
        for c in chunks:
            for cp in near_copies(c):
                cp.start()

    def relay(chunks):
        for c in chunks:
            for got, cp in zip(near_copies(c), relay_copies(c)):
                got.wait_recv()
                cp.start()

    def core_copy(t, h):
        return remote(
            u.at[t, other, h], a_recv.at[t, h], sa.at[t], ra.at[t], partner
        )

    def x_copy(t, k):
        at = pl.multiple_of(xs[k] * 64, 64)
        return remote(
            a_sum.at[t, :, pl.ds(at, 64), :], x_recv.at[t, k], sx.at[t], rx.at[t], xpeer[k]
        )

    def z_copy(t, k):
        at = pl.multiple_of(zs[k] * 8, 8)
        return remote(
            x_sum.at[t, :, pl.ds(at, 8), :], z_recv.at[t, k], sz.at[t], rz.at[t], zpeer[k]
        )

    def outer(t, left, right):
        def one(h, _):
            mat = tn(left[h], right[h])
            u[t, 0, h] = mat[:, :128]
            u[t, 1, h] = mat[:, 128:]
            core_copy(t, h).start()
            return 0

        lax.fori_loop(0, NH, one, 0)
        sent(a_recv.at[t], sa.at[t])

    def add_core(t):
        arrived(a_recv.at[t], ra.at[t])
        a_sum[t] = u[t, core] + a_recv[t]
        send([x_copy(t, k) for k in range(NX - 1)])
        sent(x_recv.at[t], sx.at[t])

    def add_x(t):
        arrived(x_recv.at[t], rx.at[t])
        mine = pl.multiple_of(x * 64, 64)
        x_sum[t] = a_sum[t, :, pl.ds(mine, 64), :] + x_recv[t, 0] + x_recv[t, 1] + x_recv[t, 2]
        send([z_copy(t, k) for k in range(NZ - 1)])
        sent(z_recv.at[t], sz.at[t])

    def add_z(t):
        arrived(z_recv.at[t], rz.at[t])
        mine = pl.multiple_of(z * 8, 8)
        total = x_sum[t, :, pl.ds(mine, 8), :]
        for k in range(NZ - 1):
            total = total + z_recv[t, k]
        full[core, t] = total

    def query_rows(qr, kr, weights, lo, hi):
        def one(i, _):
            mat = nt(weights(), sheet[pl.ds(4 * i, 4)].reshape(1024, 768))
            for n in range(4):
                sub = mat[:, 256 * n:256 * n + 256] * vm[pl.ds(4 * i + n, 1), :]
                split_rows(qr, 4 * i + n, sub[:192])
                split_rows(kr, 4 * i + n, sub[192:])
            return 0

        lax.fori_loop(lo, hi, one, 0)

    def own_weights():
        return w_t[0:384]

    def far_weights(s):
        w_c[...] = w_far[s].reshape(384, 768).T
        w_out[s + 1, :, 0:384] = w_c[rows_y, :]
        w_out[s + 1, :, 384:576] = wv_far[s].reshape(192, 192)

    def far_rows(s):
        far_weights(s)
        query_rows(q_far.at[s], k_far.at[s], lambda: w_far[s].reshape(384, 768), 0, 4)

    send(wy_copies())
    sent(w_far.at[:, 0, 0], swy.at[0])
    sent(wv_far.at[:, 0], swy.at[1])
    lax.fori_loop(2, 4, value_rows, 0)
    pltpu.make_async_copy(g_t, g_t, s_cot.at[0]).wait()
    near([0, 1, 2])
    outer(0, g_t, v_t)
    query_rows(q_t, k_t, own_weights, 0, 1)
    add_core(0)
    query_rows(q_t, k_t, own_weights, 1, 4)
    outer(1, q_t, k_t)
    near([3])
    add_core(1)
    arrived(w_far.at[:, 0, 0], rwy.at[0])
    arrived(wv_far.at[:, 0], rwy.at[1])
    send(wz_copies())
    send(wx_copies())
    sent(w_far.at[:, 0, 0], sww.at[0])
    sent(wv_far.at[:, 0], sww.at[1])
    sent(w_far.at[:, :, 0], sww.at[2])
    sent(wv_far.at[:, 0:2], sww.at[3])
    add_x(0)
    rows_y = pl.ds(pl.multiple_of(y * 192, 16), 192)
    w_c[...] = w_t[0:384].T
    w_out[0, :, 0:384] = w_c[rows_y, :]
    w_out[0, :, 384:576] = w_vc[rows_y, :]
    relay([0])
    add_x(1)
    arrived(w_far.at[:, 0, 0], rww.at[0])
    arrived(wv_far.at[:, 0], rww.at[1])
    wc_copy = remote(w_far.at[0, core], w_far.at[0, core], swc.at[0], rwc.at[0], partner)
    wd_copy = remote(w_far.at[1:3, core], w_far.at[1:3, core], swc.at[1], rwc.at[1], partner)
    send([wc_copy])
    sent(w_far.at[0, 0], swc.at[0])
    wc_copy.wait_recv()
    far_rows(0)
    add_z(0)
    add_z(1)

    half_copy = remote(full.at[core], full.at[core], sd.at[0], rd.at[0], partner)
    send([half_copy])
    sent(full.at[0], sd.at[0])
    half_copy.wait_recv()

    dprob = jnp.concatenate([full[0, 0], full[1, 0]], axis=-1)
    logits = jnp.concatenate([full[0, 1], full[1, 1]], axis=-1) * scale
    top = jnp.max(logits, axis=-1, keepdims=True)
    ex = jnp.exp(logits - top)
    probs = ex / jnp.sum(ex, axis=-1, keepdims=True)
    inner = jnp.sum(probs * dprob, axis=-1, keepdims=True)
    dscore = scale * probs * (dprob - inner)
    tile = jnp.concatenate([probs, dscore], axis=1)
    gat[core, block] = jnp.where(core == 0, tile[:, :, :128], tile[:, :, 128:]).astype(BF16)

    own = gat.at[core, block]
    gz = [remote(own, own, sgz.at[0], rgz.at[0], zpeer[k]) for k in range(NZ - 1)]
    ty = [
        remote(own, gat_far.at[k, core, block], sty.at[0], rty.at[0], ypeer[k]) for k in range(NY - 1)
    ]
    send(gz)
    send(ty)
    sent(gat.at[0, 0:7], sgz.at[0])
    sent(gat_far.at[:, 0, 0], sty.at[0])
    near([4, 5, 6, 7])

    xblock = pl.ds(pl.multiple_of(x * NZ, NZ), NZ)

    def gx_copy(k):
        src = gat.at[core, xblock]
        return remote(src, src, sgx.at[0], rgx.at[k], xpeer[k])

    def from_x(k):
        return pl.ds(pl.multiple_of(lax.rem(x + NX - k, NX) * NZ, NZ), NZ)

    def gc_copy(k):
        src = gat.at[core, from_x(k)]
        return remote(src, src, sgc.at[0], rgc.at[0], partner)

    def oz_copy(k):
        src = gat_far.at[:, core, block]
        return remote(src, src, soz.at[0], roz.at[0], zpeer[k])

    def ox_copy(s, k):
        src = gat_far.at[s, core, xblock]
        return remote(src, src, sox.at[0], rox.at[s], xpeer[k])

    def oc_copy(s, k):
        src = gat_far.at[s, core, from_x(k)]
        return remote(src, src, soc.at[0], roc.at[s], partner)

    arrived(w_far.at[:, :, 0], rww.at[2])
    arrived(wv_far.at[:, 0:2], rww.at[3])
    send([wd_copy])
    sent(w_far.at[1:3, 0], swc.at[1])
    arrived(gat.at[0, 0:7], rgz.at[0])
    send([gx_copy(k) for k in range(NX - 1)])
    send([gc_copy(0)])
    arrived(gat_far.at[:, 0, 0], rty.at[0])
    send([oz_copy(k) for k in range(NZ - 1)])
    wd_copy.wait_recv()
    far_rows(1)
    far_rows(2)
    relay([1, 2])
    for k in range(NX - 1):
        gx_copy(k).wait_recv()
        send([gc_copy(k + 1)])
    sent(gat.at[0, 0:24], sgx.at[0])
    sent(gat.at[0], sgc.at[0])
    arrived(gat.at[0], rgc.at[0])

    def unpack(src):
        def one(h, _):
            for ch in range(2):
                mat = src(ch, h).astype(F32)
                prob[h, :, ch * 128:(ch + 1) * 128] = mat[:, :8].reshape(256, 128).astype(BF16)
                dsc[h, :, ch * 128:(ch + 1) * 128] = mat[:, 8:].reshape(256, 128).astype(BF16)
            return 0

        lax.fori_loop(0, NH, one, 0)

    def masked(ref, h, mat):
        for r in range(16):
            ref[h, r * 64:(r + 1) * 64, :] = (mat[r * 64:(r + 1) * 64] * vm[r:r + 1, :]).astype(BF16)

    def back_qk(qr, kr):
        def one(h, _):
            dq = nt(kr[h], dsc[h])
            dk = nn(qr[h], dsc[h])
            masked(qr, h, dq)
            masked(kr, h, dk)
            return 0

        lax.fori_loop(0, NH, one, 0)

    def gathered(refs, c):
        cols = []
        for n in range(4):
            at = pl.multiple_of(c * 256 + n * 64, 64)
            cols.append(jnp.concatenate([ref[h, pl.ds(at, 64), :] for ref in refs for h in range(NH)], axis=0))
        return jnp.concatenate(cols, axis=1)

    unpack(lambda ch, h: gat[ch, :, h])
    back_qk(q_t, k_t)

    def back_v(h, _):
        masked(v_t, h, nn(g_t[h], prob[h]))
        return 0

    lax.fori_loop(0, NH, back_v, 0)
    arrived(gat_far.at[:, 0, 0:7], roz.at[0])
    sent(gat_far.at[:, 0, 0:7], soz.at[0])
    send([ox_copy(s, k) for s in (0, 2, 1) for k in range(NX - 1)])
    send([oc_copy(s, 0) for s in range(NY - 1)])
    sent(gat_far.at[:, 0, 0:24], sox.at[0])
    sent(gat_far.at[:, 0], soc.at[0])
    relay([3])
    wg_acc[...] = jnp.zeros_like(wg_acc)

    def own_wg(c, _):
        wg_acc[...] += nn(gathered((q_t, k_t, v_t), c), sheet[pl.ds(4 * c, 4)].reshape(1024, 768))
        return 0

    def own_out(c, _):
        acc[c] = nn(w_out[0], gathered((q_t, k_t, v_t), c))
        return 0

    lax.fori_loop(0, 4, own_wg, 0)
    wg_n[...] = wg_acc[...].T
    for gc in range(2):
        for gz_ in range(NZ):
            rows = [wg_n[12 * g:12 * g + 12, :] for g in range(8 * gz_ + gc, 8 * gz_ + 8, 2)]
            wg_b[gc, gz_] = jnp.concatenate(rows, axis=0).astype(BF16)
    wa = remote(wg_b.at[other], wa_recv, swa.at[0], rwa.at[0], partner)
    send([wa])
    sent(wa_recv, swa.at[0])
    relay([4, 5])
    lax.fori_loop(0, 4, own_out, 0)

    def far_ready(s):
        arrived(gat_far.at[s, 0, 0:24], rox.at[s])
        send([oc_copy(s, k + 1) for k in range(NX - 1)])

    def wz_copy(k):
        return remote(wa_recv.at[zs[k]], wz_recv.at[k], swz.at[0], rwz.at[0], zpeer[k])

    def wx_copy(k):
        return remote(wx_sum.at[xs[k]], wx_recv.at[k], swx.at[0], rwx.at[0], xpeer[k])

    def far_qk(s):
        arrived(gat_far.at[s, 0], roc.at[s])
        unpack(lambda ch, h: gat_far[s, ch, :, h])
        back_qk(q_far.at[s], k_far.at[s])

    def far_qk_out(s):
        def one(c, _):
            acc[c] += nn(w_out[s + 1, :, 0:384], gathered((q_far.at[s], k_far.at[s]), c))
            return 0

        lax.fori_loop(0, 4, one, 0)

    def far_v(s, h, c):
        at = pl.multiple_of(c * 256, 256)
        mat = nn(g_far[s, h, pl.ds(at, 256), :], prob[h])
        return [
            (mat[n * 64:(n + 1) * 64] * vm[pl.ds(4 * c + n, 1), :]).astype(BF16) for n in range(4)
        ]

    def far_v_mat(s, c):
        parts = [far_v(s, h, c) for h in range(NH)]
        return jnp.concatenate(
            [jnp.concatenate([parts[h][n] for h in range(NH)], axis=0) for n in range(4)], axis=1
        )

    def far_out(s, lo, hi):
        def one(c, _):
            grads = jnp.concatenate([gathered((q_far.at[s], k_far.at[s]), c), far_v_mat(s, c)], axis=0)
            acc[c] += nn(w_out[s + 1], grads)
            return 0

        lax.fori_loop(lo, hi, one, 0)

    wa.wait_recv()
    wa_recv[...] = (wa_recv[...].astype(F32) + wg_b[core].astype(F32)).astype(BF16)
    send([wz_copy(k) for k in range(NZ - 1)])
    sent(wz_recv, swz.at[0])
    far_ready(0)
    far_qk(0)
    relay([6, 7])
    far_out(0, 0, 2)
    far_ready(2)
    far_out(0, 2, 4)
    far_qk(2)
    far_out(2, 0, 3)
    far_ready(1)
    far_out(2, 3, 4)
    far_qk(1)
    arrived(wz_recv, rwz.at[0])
    wsum = wa_recv[z].astype(F32)
    for k in range(NZ - 1):
        wsum = wsum + wz_recv[k].astype(F32)
    wx_f[0:48] = wsum
    wx_f[48:56] = jnp.zeros((8, 576), F32)
    for n in range(NX):
        wx_sum[n] = wx_f[12 * n:12 * n + 16, :].astype(BF16)
    send([wx_copy(k) for k in range(NX - 1)])
    sent(wx_recv, swx.at[0])

    far_qk_out(1)

    def out_copy(c):
        rows = pl.ds(4 * c, 4)
        return pltpu.make_async_copy(out_v.at[rows], out_h.at[rows], s_out.at[0])

    for c in range(4):
        arrived(g_far.at[1, :, 256 * c:256 * c + 256, :], rgr.at[c])
        tot = acc[c] + nn(w_out[2, :, 384:576], far_v_mat(1, c))
        for n in range(4):
            out_v[4 * c + n] = tot[:, 256 * n:256 * n + 256].astype(BF16)
        out_copy(c).start()

    arrived(wx_recv, rwx.at[0])
    total = wx_sum[x].astype(F32)
    for k in range(NX - 1):
        total = total + wx_recv[k].astype(F32)
    for t in range(3):
        wg_out[:, t, :] = total[:12, 192 * t:192 * t + 192]

    for n in range(2):
        sent(g_t, sg.at[n])
        sent(g_far.at[1, :, 0:512, :], sgr.at[n])
    flush()
    pltpu.make_async_copy(out_v, out_v, s_out.at[0]).wait()


def place(out_h, wg_h, out_f, wg_f, out_v, wg_v, s_in, s_out):
    def pieces(src, dst, sem):
        got = [pltpu.make_async_copy(src[1], dst[1], sem.at[4])]
        for c in range(4):
            rows = pl.ds(4 * c, 4)
            got.append(pltpu.make_async_copy(src[0].at[rows], dst[0].at[rows], sem.at[c]))
        return got

    first = pieces((out_h, wg_h), (out_v, wg_v), s_in)
    second = pieces((out_v, wg_v), (out_f, wg_f), s_out)
    for c in first:
        c.start()
    for a, b in zip(first, second):
        a.wait()
        b.start()
    for c in second:
        c.wait()


def body(sheet, w_query, w_key, w_value, cotangent, lengths):
    scale = float((HEAD_DIM * sheet.shape[0] * lax.axis_size("rows")) ** -0.5)
    vmem = pl.BlockSpec(memory_space=pltpu.VMEM)
    anyw = pl.BlockSpec(memory_space=pl.ANY)
    dma = pltpu.SemaphoreType.DMA
    V = pltpu.VMEM
    rows = (3, 1024, 256)
    scratch = [
        V((16, 256, 768), BF16), V((576, 768), BF16), V((768, 384), BF16), V((768, 192), BF16), V((16, 256), F32),
        V(rows, BF16), V(rows, BF16), V(rows, BF16), V(rows, BF16),
        V((3, 2, 4, 48, 768), BF16), V((3, 4, 48, 192), BF16), V((4, 192, 576), BF16),
        V((3,) + rows, BF16), V((3,) + rows, BF16), V((3,) + rows, BF16),
        V((2, 2, 3, 256, 128), F32), V((2, 3, 256, 128), F32), V((2, 3, 256, 128), F32),
        V((2, 3, 3, 64, 128), F32), V((2, 3, 64, 128), F32),
        V((2, 7, 3, 8, 128), F32), V((2, 2, 3, 8, 128), F32),
        V((2, 32, 3, 16, 128), BF16), V((3, 2, 32, 3, 16, 128), BF16),
        V((3, 256, 256), BF16), V((3, 256, 256), BF16),
        V((4, 192, 1024), F32), V((16, 192, 256), BF16),
        V((576, 768), F32), V((768, 576), F32), V((2, 8, 48, 576), BF16), V((8, 48, 576), BF16),
        V((7, 48, 576), BF16), V((56, 576), F32), V((4, 16, 576), BF16), V((3, 16, 576), BF16),
        dma((4,)), dma((1,)), dma((1,)), dma((1,)),
    ]
    shapes = [
        (2, 2), (2, 2), (2, 2), (1, 1), (1, 1), (1, 3), (1, 1),
        (2, 2), (4, 4), (2, 2), (2, (2, 8)), (2, 4), (1, 1), (1, 1), (1, 3), (1, 3),
        (1, 1), (1, 1), (1, 1),
    ]
    for out_shape, in_shape in shapes:
        scratch += [dma(shape if isinstance(shape, tuple) else (shape,)) for shape in (out_shape, in_shape)]
    out, wg = pl.pallas_call(
        functools.partial(kernel, scale),
        out_shape=(jax.ShapeDtypeStruct((16, 192, 256), BF16), jax.ShapeDtypeStruct((12, 3, 192), F32)),
        in_specs=[anyw] * 5 + [pl.BlockSpec(memory_space=pltpu.SMEM)],
        out_specs=(anyw, vmem),
        scratch_shapes=scratch,
        compiler_params=pltpu.CompilerParams(
            collective_id=0, has_side_effects=True, vmem_limit_bytes=62 * 1024 * 1024
        ),
    )(
        sheet, w_query.T, w_key.T, w_value.T,
        cotangent.transpose(0, 2, 1).reshape(16, NH, HEAD_DIM, 256), lengths,
    )
    out, wg = pl.pallas_call(
        place,
        out_shape=(jax.ShapeDtypeStruct(out.shape, BF16), jax.ShapeDtypeStruct(wg.shape, F32)),
        in_specs=[anyw, anyw],
        out_specs=(anyw, anyw),
        scratch_shapes=[V(out.shape, BF16), V(wg.shape, F32), dma((5,)), dma((5,))],
    )(out, wg)
    return out.transpose(0, 2, 1), wg


def solution(mesh):
    in_specs = (
        P("rows", None, None),
        P(None, "heads"),
        P(None, "heads"),
        P(None, "heads"),
        P("rows", None, "heads"),
        P("rows"),
    )
    out_specs = (P("rows", None, "heads"), P("rows", None, "heads"))
    return jax.shard_map(body, mesh=mesh, in_specs=in_specs, out_specs=out_specs, check_vma=False)
```

```python
import functools

import jax
import jax.numpy as jnp
from jax import lax
from jax.experimental import pallas as pl
from jax.experimental.pallas import tpu as pltpu
from jax.sharding import PartitionSpec as P

HEAD_DIM = 64
MESH = pl.DeviceIdType.MESH
NX, NZ, NY = 4, 8, 4
NH = 3
F32 = jnp.float32
BF16 = jnp.bfloat16


def nt(a, b):
    return lax.dot_general(a, b, (((1,), (1,)), ((), ())), preferred_element_type=F32)


def nn(a, b):
    return lax.dot_general(a, b, (((1,), (0,)), ((), ())), preferred_element_type=F32)


def tn(a, b):
    return lax.dot_general(a, b, (((0,), (0,)), ((), ())), preferred_element_type=F32)


def kernel(
    scale,
    sheet_h, wq, wk, wv, cot_h, lens, out_h, wg_out,
    sheet, w_t, w_c, w_vc, vm, q_t, k_t, v_t, g_t,
    w_far, wv_far, w_out, q_far, k_far, g_far,
    u, a_recv, a_sum, x_recv, x_sum, z_recv, full, gat, gat_far, prob, dsc,
    acc, out_v, wg_acc, wg_n, wg_b, wa_recv, wz_recv, wx_f, wx_sum, wx_recv,
    s_sheet, s_cot, s_w, s_out,
    sa, ra, sx, rx, sz, rz, sd, rd, sgz, rgz, sgx, rgx, sgc, rgc,
    swy, rwy, sww, rww, swc, rwc, sg, rg, sgr, rgr, sty, rty, soz, roz, sox, rox, soc, roc,
    swa, rwa, swx, rwx, swz, rwz,
):
    ri = lax.axis_index("rows")
    y = lax.axis_index("heads")
    core = lax.rem(ri, 2)
    x = lax.rem(ri // 2, NX)
    z = ri // (2 * NX)
    other = 1 - core
    block = x * NZ + z
    partner = {"rows": (z * NX + x) * 2 + other}
    xs = [lax.rem(x + k, NX) for k in range(1, NX)]
    zs = [lax.rem(z + k, NZ) for k in range(1, NZ)]
    ys = [lax.rem(y + k, NY) for k in range(1, NY)]
    xpeer = [{"rows": (z * NX + xk) * 2 + core} for xk in xs]
    zpeer = [{"rows": (zk * NX + x) * 2 + core} for zk in zs]
    ypeer = [{"heads": yk} for yk in ys]
    d_up, d_dn = ypeer[0], ypeer[2]

    def remote(src, dst, ss, rs, dev):
        return pltpu.make_async_remote_copy(
            src_ref=src, dst_ref=dst, send_sem=ss, recv_sem=rs, device_id=dev, device_id_type=MESH
        )

    sends = []

    def send(copies):
        for c in copies:
            c.start()

    def sent(ref, sem):
        sends.append((ref, sem))

    def flush():
        for ref, sem in sends:
            remote(ref, ref, sem, sem, partner).wait_send()

    def arrived(ref, sem):
        remote(ref, ref, sem, sem, partner).wait_recv()

    def w_copy(t):
        return pltpu.make_async_copy((wq, wk, wv)[t], w_t.at[192 * t:192 * t + 192], s_w.at[0])

    def sheet_copy(i):
        rows = pl.ds(4 * i, 4)
        return pltpu.make_async_copy(sheet_h.at[rows], sheet.at[rows], s_sheet.at[i])

    def cot_copy(r):
        return pltpu.make_async_copy(cot_h.at[r], g_t.at[:, 64 * r:64 * r + 64, :], s_cot.at[0])

    for t in range(3):
        w_copy(t).start()
    sheet_copy(0).start()

    barrier = pltpu.get_barrier_semaphore()
    peers = [partner] + ypeer + xpeer + zpeer
    for dev in peers:
        pl.semaphore_signal(barrier, inc=1, device_id=dev, device_id_type=MESH)

    for r in range(16):
        vm[r:r + 1, :] = (lax.broadcasted_iota(jnp.int32, (1, 256), 1) < lens[r]).astype(F32)

    def split_rows(ref, r, mat):
        at = pl.multiple_of(r * 64, 64)
        for h in range(NH):
            ref[h, pl.ds(at, 64), :] = mat[h * 64:(h + 1) * 64].astype(BF16)

    def value_rows(i, _):
        sheet_copy(i).wait()
        mat = nt(w_t[384:576], sheet[pl.ds(4 * i, 4)].reshape(1024, 768))
        for n in range(4):
            split_rows(v_t, 4 * i + n, mat[:, 256 * n:256 * n + 256] * vm[pl.ds(4 * i + n, 1), :])
        return 0

    pltpu.make_async_copy(w_t, w_t, s_w.at[0]).wait()
    for i in range(1, 4):
        sheet_copy(i).start()
    for r in range(16):
        cot_copy(r).start()
    w_vc[...] = w_t[384:576].T
    lax.fori_loop(0, 2, value_rows, 0)
    pl.semaphore_wait(barrier, len(peers))

    quarter = lax.rem(z, 4)
    piece = [quarter, x, x]

    def wy_copies():
        got = []
        for k in range(NY - 1):
            p = piece[k]
            src = w_t.at[pl.ds(pl.multiple_of(core * 192 + p * 48, 16), 48), :]
            got.append(remote(src, w_far.at[k, core, p], swy.at[0], rwy.at[0], ypeer[k]))
            src = w_vc.at[pl.ds(pl.multiple_of(ys[k] * 192 + p * 48, 16), 48), :]
            got.append(remote(src, wv_far.at[k, p], swy.at[1], rwy.at[1], ypeer[k]))
        return got

    hop2 = lax.rem(z + 2 + 4 * lax.rem(z, 2), NZ)
    wpeer = [zpeer[0], zpeer[NZ - 2], {"rows": (hop2 * NX + x) * 2 + core}]

    def wz_copies():
        got = []
        for k in range(3):
            ref = w_far.at[0, core, quarter]
            got.append(remote(ref, ref, sww.at[0], rww.at[0], wpeer[k]))
            ref = wv_far.at[0, quarter]
            got.append(remote(ref, ref, sww.at[1], rww.at[1], wpeer[k]))
        return got

    def wx_copies():
        got = []
        for k in range(3):
            ref = w_far.at[1:3, core, x]
            got.append(remote(ref, ref, sww.at[2], rww.at[2], xpeer[k]))
            ref = wv_far.at[1:3, x]
            got.append(remote(ref, ref, sww.at[3], rww.at[3], xpeer[k]))
        return got

    def near_copies(c):
        src = g_t.at[:, 128 * c:128 * c + 128, :]
        return [
            remote(src, g_far.at[0, :, 128 * c:128 * c + 128, :], sg.at[0], rg.at[0, c], d_up),
            remote(src, g_far.at[2, :, 128 * c:128 * c + 128, :], sg.at[1], rg.at[1, c], d_dn),
        ]

    def relay_copies(c):
        lo, hi = 128 * c, 128 * c + 64
        return [
            remote(
                g_far.at[0, :, lo:lo + 64, :], g_far.at[1, :, lo:lo + 64, :], sgr.at[0], rgr.at[c // 2], d_up
            ),
            remote(
                g_far.at[2, :, hi:hi + 64, :], g_far.at[1, :, hi:hi + 64, :], sgr.at[1], rgr.at[c // 2], d_dn
            ),
        ]

    def near(chunks):
        for c in chunks:
            for cp in near_copies(c):
                cp.start()

    def relay(chunks):
        for c in chunks:
            for got, cp in zip(near_copies(c), relay_copies(c)):
                got.wait_recv()
                cp.start()

    def core_copy(t, h):
        return remote(
            u.at[t, other, h], a_recv.at[t, h], sa.at[t], ra.at[t], partner
        )

    def x_copy(t, k):
        at = pl.multiple_of(xs[k] * 64, 64)
        return remote(
            a_sum.at[t, :, pl.ds(at, 64), :], x_recv.at[t, k], sx.at[t], rx.at[t], xpeer[k]
        )

    def z_copy(t, k):
        at = pl.multiple_of(zs[k] * 8, 8)
        return remote(
            x_sum.at[t, :, pl.ds(at, 8), :], z_recv.at[t, k], sz.at[t], rz.at[t], zpeer[k]
        )

    def outer(t, left, right):
        def one(h, _):
            mat = tn(left[h], right[h])
            u[t, 0, h] = mat[:, :128]
            u[t, 1, h] = mat[:, 128:]
            core_copy(t, h).start()
            return 0

        lax.fori_loop(0, NH, one, 0)
        sent(a_recv.at[t], sa.at[t])

    def add_core(t):
        arrived(a_recv.at[t], ra.at[t])
        a_sum[t] = u[t, core] + a_recv[t]
        send([x_copy(t, k) for k in range(NX - 1)])
        sent(x_recv.at[t], sx.at[t])

    def add_x(t):
        arrived(x_recv.at[t], rx.at[t])
        mine = pl.multiple_of(x * 64, 64)
        x_sum[t] = a_sum[t, :, pl.ds(mine, 64), :] + x_recv[t, 0] + x_recv[t, 1] + x_recv[t, 2]
        send([z_copy(t, k) for k in range(NZ - 1)])
        sent(z_recv.at[t], sz.at[t])

    def add_z(t):
        arrived(z_recv.at[t], rz.at[t])
        mine = pl.multiple_of(z * 8, 8)
        total = x_sum[t, :, pl.ds(mine, 8), :]
        for k in range(NZ - 1):
            total = total + z_recv[t, k]
        full[core, t] = total

    def query_rows(qr, kr, weights, lo, hi):
        def one(i, _):
            mat = nt(weights(), sheet[pl.ds(4 * i, 4)].reshape(1024, 768))
            for n in range(4):
                sub = mat[:, 256 * n:256 * n + 256] * vm[pl.ds(4 * i + n, 1), :]
                split_rows(qr, 4 * i + n, sub[:192])
                split_rows(kr, 4 * i + n, sub[192:])
            return 0

        lax.fori_loop(lo, hi, one, 0)

    def own_weights():
        return w_t[0:384]

    def far_weights(s):
        w_c[...] = w_far[s].reshape(384, 768).T
        w_out[s + 1, :, 0:384] = w_c[rows_y, :]
        w_out[s + 1, :, 384:576] = wv_far[s].reshape(192, 192)

    def far_rows(s):
        far_weights(s)
        query_rows(q_far.at[s], k_far.at[s], lambda: w_far[s].reshape(384, 768), 0, 4)

    send(wy_copies())
    sent(w_far.at[:, 0, 0], swy.at[0])
    sent(wv_far.at[:, 0], swy.at[1])
    lax.fori_loop(2, 4, value_rows, 0)
    pltpu.make_async_copy(g_t, g_t, s_cot.at[0]).wait()
    outer(0, g_t, v_t)
    query_rows(q_t, k_t, own_weights, 0, 1)
    add_core(0)
    query_rows(q_t, k_t, own_weights, 1, 4)
    outer(1, q_t, k_t)
    arrived(w_far.at[:, 0, 0], rwy.at[0])
    arrived(wv_far.at[:, 0], rwy.at[1])
    send(wz_copies())
    near([0, 1, 2])
    add_core(1)
    send(wx_copies())
    sent(w_far.at[:, 0, 0], sww.at[0])
    sent(wv_far.at[:, 0], sww.at[1])
    sent(w_far.at[:, :, 0], sww.at[2])
    sent(wv_far.at[:, 0:2], sww.at[3])
    add_x(0)
    rows_y = pl.ds(pl.multiple_of(y * 192, 16), 192)
    w_c[...] = w_t[0:384].T
    w_out[0, :, 0:384] = w_c[rows_y, :]
    w_out[0, :, 384:576] = w_vc[rows_y, :]
    add_x(1)
    relay([0])
    arrived(w_far.at[:, 0, 0], rww.at[0])
    arrived(wv_far.at[:, 0], rww.at[1])
    wc_copy = remote(w_far.at[0, core], w_far.at[0, core], swc.at[0], rwc.at[0], partner)
    wd_copy = remote(w_far.at[1:3, core], w_far.at[1:3, core], swc.at[1], rwc.at[1], partner)
    send([wc_copy])
    sent(w_far.at[0, 0], swc.at[0])
    wc_copy.wait_recv()
    far_rows(0)
    relay([1])
    add_z(0)
    add_z(1)

    half_copy = remote(full.at[core], full.at[core], sd.at[0], rd.at[0], partner)
    send([half_copy])
    sent(full.at[0], sd.at[0])
    half_copy.wait_recv()

    dprob = jnp.concatenate([full[0, 0], full[1, 0]], axis=-1)
    logits = jnp.concatenate([full[0, 1], full[1, 1]], axis=-1) * scale
    top = jnp.max(logits, axis=-1, keepdims=True)
    ex = jnp.exp(logits - top)
    probs = ex / jnp.sum(ex, axis=-1, keepdims=True)
    inner = jnp.sum(probs * dprob, axis=-1, keepdims=True)
    dscore = scale * probs * (dprob - inner)
    tile = jnp.concatenate([probs, dscore], axis=1)
    gat[core, block] = jnp.where(core == 0, tile[:, :, :128], tile[:, :, 128:]).astype(BF16)

    own = gat.at[core, block]
    gz = [remote(own, own, sgz.at[0], rgz.at[0], zpeer[k]) for k in range(NZ - 1)]
    ty = [
        remote(own, gat_far.at[k, core, block], sty.at[0], rty.at[0], ypeer[k]) for k in range(NY - 1)
    ]
    send(gz)
    send(ty)
    sent(gat.at[0, 0:7], sgz.at[0])
    sent(gat_far.at[:, 0, 0], sty.at[0])
    near([3, 4, 5, 6, 7])

    xblock = pl.ds(pl.multiple_of(x * NZ, NZ), NZ)

    def gx_copy(k):
        src = gat.at[core, xblock]
        return remote(src, src, sgx.at[0], rgx.at[k], xpeer[k])

    def from_x(k):
        return pl.ds(pl.multiple_of(lax.rem(x + NX - k, NX) * NZ, NZ), NZ)

    def gc_copy(k):
        src = gat.at[core, from_x(k)]
        return remote(src, src, sgc.at[0], rgc.at[0], partner)

    def oz_copy(k):
        src = gat_far.at[:, core, block]
        return remote(src, src, soz.at[0], roz.at[0], zpeer[k])

    def ox_copy(s, k):
        src = gat_far.at[s, core, xblock]
        return remote(src, src, sox.at[0], rox.at[s], xpeer[k])

    def oc_copy(s, k):
        src = gat_far.at[s, core, from_x(k)]
        return remote(src, src, soc.at[0], roc.at[s], partner)

    arrived(w_far.at[:, :, 0], rww.at[2])
    arrived(wv_far.at[:, 0:2], rww.at[3])
    send([wd_copy])
    sent(w_far.at[1:3, 0], swc.at[1])
    wd_copy.wait_recv()
    far_rows(1)
    arrived(gat.at[0, 0:7], rgz.at[0])
    send([gx_copy(k) for k in range(NX - 1)])
    send([gc_copy(0)])
    arrived(gat_far.at[:, 0, 0], rty.at[0])
    send([oz_copy(k) for k in range(NZ - 1)])
    far_rows(2)
    relay([2])
    for k in range(NX - 1):
        gx_copy(k).wait_recv()
        send([gc_copy(k + 1)])
    sent(gat.at[0, 0:24], sgx.at[0])
    sent(gat.at[0], sgc.at[0])
    arrived(gat.at[0], rgc.at[0])

    def unpack(src):
        def one(h, _):
            for ch in range(2):
                mat = src(ch, h).astype(F32)
                prob[h, :, ch * 128:(ch + 1) * 128] = mat[:, :8].reshape(256, 128).astype(BF16)
                dsc[h, :, ch * 128:(ch + 1) * 128] = mat[:, 8:].reshape(256, 128).astype(BF16)
            return 0

        lax.fori_loop(0, NH, one, 0)

    def masked(ref, h, mat):
        for r in range(16):
            ref[h, r * 64:(r + 1) * 64, :] = (mat[r * 64:(r + 1) * 64] * vm[r:r + 1, :]).astype(BF16)

    def back_qk(qr, kr):
        def one(h, _):
            dq = nt(kr[h], dsc[h])
            dk = nn(qr[h], dsc[h])
            masked(qr, h, dq)
            masked(kr, h, dk)
            return 0

        lax.fori_loop(0, NH, one, 0)

    def gathered(refs, c):
        cols = []
        for n in range(4):
            at = pl.multiple_of(c * 256 + n * 64, 64)
            cols.append(jnp.concatenate([ref[h, pl.ds(at, 64), :] for ref in refs for h in range(NH)], axis=0))
        return jnp.concatenate(cols, axis=1)

    unpack(lambda ch, h: gat[ch, :, h])
    back_qk(q_t, k_t)

    def back_v(h, _):
        masked(v_t, h, nn(g_t[h], prob[h]))
        return 0

    lax.fori_loop(0, NH, back_v, 0)
    arrived(gat_far.at[:, 0, 0:7], roz.at[0])
    sent(gat_far.at[:, 0, 0:7], soz.at[0])
    send([ox_copy(s, k) for s in (0, 2, 1) for k in range(NX - 1)])
    send([oc_copy(s, 0) for s in range(NY - 1)])
    sent(gat_far.at[:, 0, 0:24], sox.at[0])
    sent(gat_far.at[:, 0], soc.at[0])
    relay([3])
    wg_acc[...] = jnp.zeros_like(wg_acc)

    def own_wg(c, _):
        wg_acc[...] += nn(gathered((q_t, k_t, v_t), c), sheet[pl.ds(4 * c, 4)].reshape(1024, 768))
        return 0

    def own_out(c, _):
        acc[c] = nn(w_out[0], gathered((q_t, k_t, v_t), c))
        return 0

    lax.fori_loop(0, 4, own_wg, 0)
    wg_n[...] = wg_acc[...].T
    for gc in range(2):
        for gz_ in range(NZ):
            rows = [wg_n[12 * g:12 * g + 12, :] for g in range(8 * gz_ + gc, 8 * gz_ + 8, 2)]
            wg_b[gc, gz_] = jnp.concatenate(rows, axis=0).astype(BF16)
    wa = remote(wg_b.at[other], wa_recv, swa.at[0], rwa.at[0], partner)
    send([wa])
    sent(wa_recv, swa.at[0])
    relay([4, 5])
    lax.fori_loop(0, 4, own_out, 0)

    def far_ready(s):
        arrived(gat_far.at[s, 0, 0:24], rox.at[s])
        send([oc_copy(s, k + 1) for k in range(NX - 1)])

    def wz_copy(k):
        return remote(wa_recv.at[zs[k]], wz_recv.at[k], swz.at[0], rwz.at[0], zpeer[k])

    def wx_copy(k):
        return remote(wx_sum.at[xs[k]], wx_recv.at[k], swx.at[0], rwx.at[0], xpeer[k])

    def far_qk(s):
        arrived(gat_far.at[s, 0], roc.at[s])
        unpack(lambda ch, h: gat_far[s, ch, :, h])
        back_qk(q_far.at[s], k_far.at[s])

    def far_v(s, h, c):
        at = pl.multiple_of(c * 256, 256)
        mat = nn(g_far[s, h, pl.ds(at, 256), :], prob[h])
        return [
            (mat[n * 64:(n + 1) * 64] * vm[pl.ds(4 * c + n, 1), :]).astype(BF16) for n in range(4)
        ]

    def far_v_mat(s, c):
        parts = [far_v(s, h, c) for h in range(NH)]
        return jnp.concatenate(
            [jnp.concatenate([parts[h][n] for h in range(NH)], axis=0) for n in range(4)], axis=1
        )

    def far_out(s, lo, hi):
        def one(c, _):
            grads = jnp.concatenate([gathered((q_far.at[s], k_far.at[s]), c), far_v_mat(s, c)], axis=0)
            acc[c] += nn(w_out[s + 1], grads)
            return 0

        lax.fori_loop(lo, hi, one, 0)

    wa.wait_recv()
    wa_recv[...] = (wa_recv[...].astype(F32) + wg_b[core].astype(F32)).astype(BF16)
    send([wz_copy(k) for k in range(NZ - 1)])
    sent(wz_recv, swz.at[0])
    far_ready(0)
    far_qk(0)
    relay([6, 7])
    far_out(0, 0, 2)
    far_ready(2)
    far_out(0, 2, 4)
    far_qk(2)
    far_out(2, 0, 3)
    far_ready(1)
    far_out(2, 3, 4)
    far_qk(1)
    arrived(wz_recv, rwz.at[0])
    wsum = wa_recv[z].astype(F32)
    for k in range(NZ - 1):
        wsum = wsum + wz_recv[k].astype(F32)
    wx_f[0:48] = wsum
    wx_f[48:56] = jnp.zeros((8, 576), F32)
    for n in range(NX):
        wx_sum[n] = wx_f[12 * n:12 * n + 16, :].astype(BF16)
    send([wx_copy(k) for k in range(NX - 1)])
    sent(wx_recv, swx.at[0])


    def out_copy(c):
        rows = pl.ds(4 * c, 4)
        return pltpu.make_async_copy(out_v.at[rows], out_h.at[rows], s_out.at[0])

    for c in range(4):
        arrived(g_far.at[1, :, 256 * c:256 * c + 256, :], rgr.at[c])
        grads = jnp.concatenate([gathered((q_far.at[1], k_far.at[1]), c), far_v_mat(1, c)], axis=0)
        tot = acc[c] + nn(w_out[2], grads)
        for n in range(4):
            out_v[4 * c + n] = tot[:, 256 * n:256 * n + 256].astype(BF16)
        out_copy(c).start()

    arrived(wx_recv, rwx.at[0])
    total = wx_sum[x].astype(F32)
    for k in range(NX - 1):
        total = total + wx_recv[k].astype(F32)
    for t in range(3):
        wg_out[:, t, :] = total[:12, 192 * t:192 * t + 192]

    for n in range(2):
        sent(g_t, sg.at[n])
        sent(g_far.at[1, :, 0:512, :], sgr.at[n])
    flush()
    pltpu.make_async_copy(out_v, out_v, s_out.at[0]).wait()


def place(out_h, wg_h, out_f, wg_f, out_v, wg_v, s_in, s_out):
    def pieces(src, dst, sem):
        got = [pltpu.make_async_copy(src[1], dst[1], sem.at[4])]
        for c in range(4):
            rows = pl.ds(4 * c, 4)
            got.append(pltpu.make_async_copy(src[0].at[rows], dst[0].at[rows], sem.at[c]))
        return got

    first = pieces((out_h, wg_h), (out_v, wg_v), s_in)
    second = pieces((out_v, wg_v), (out_f, wg_f), s_out)
    for c in first:
        c.start()
    for a, b in zip(first, second):
        a.wait()
        b.start()
    for c in second:
        c.wait()


def body(sheet, w_query, w_key, w_value, cotangent, lengths):
    scale = float((HEAD_DIM * sheet.shape[0] * lax.axis_size("rows")) ** -0.5)
    vmem = pl.BlockSpec(memory_space=pltpu.VMEM)
    anyw = pl.BlockSpec(memory_space=pl.ANY)
    dma = pltpu.SemaphoreType.DMA
    V = pltpu.VMEM
    rows = (3, 1024, 256)
    scratch = [
        V((16, 256, 768), BF16), V((576, 768), BF16), V((768, 384), BF16), V((768, 192), BF16), V((16, 256), F32),
        V(rows, BF16), V(rows, BF16), V(rows, BF16), V(rows, BF16),
        V((3, 2, 4, 48, 768), BF16), V((3, 4, 48, 192), BF16), V((4, 192, 576), BF16),
        V((3,) + rows, BF16), V((3,) + rows, BF16), V((3,) + rows, BF16),
        V((2, 2, 3, 256, 128), F32), V((2, 3, 256, 128), F32), V((2, 3, 256, 128), F32),
        V((2, 3, 3, 64, 128), F32), V((2, 3, 64, 128), F32),
        V((2, 7, 3, 8, 128), F32), V((2, 2, 3, 8, 128), F32),
        V((2, 32, 3, 16, 128), BF16), V((3, 2, 32, 3, 16, 128), BF16),
        V((3, 256, 256), BF16), V((3, 256, 256), BF16),
        V((4, 192, 1024), F32), V((16, 192, 256), BF16),
        V((576, 768), F32), V((768, 576), F32), V((2, 8, 48, 576), BF16), V((8, 48, 576), BF16),
        V((7, 48, 576), BF16), V((56, 576), F32), V((4, 16, 576), BF16), V((3, 16, 576), BF16),
        dma((4,)), dma((1,)), dma((1,)), dma((1,)),
    ]
    shapes = [
        (2, 2), (2, 2), (2, 2), (1, 1), (1, 1), (1, 3), (1, 1),
        (2, 2), (4, 4), (2, 2), (2, (2, 8)), (2, 4), (1, 1), (1, 1), (1, 3), (1, 3),
        (1, 1), (1, 1), (1, 1),
    ]
    for out_shape, in_shape in shapes:
        scratch += [dma(shape if isinstance(shape, tuple) else (shape,)) for shape in (out_shape, in_shape)]
    out, wg = pl.pallas_call(
        functools.partial(kernel, scale),
        out_shape=(jax.ShapeDtypeStruct((16, 192, 256), BF16), jax.ShapeDtypeStruct((12, 3, 192), F32)),
        in_specs=[anyw] * 5 + [pl.BlockSpec(memory_space=pltpu.SMEM)],
        out_specs=(anyw, vmem),
        scratch_shapes=scratch,
        compiler_params=pltpu.CompilerParams(
            collective_id=0, has_side_effects=True, vmem_limit_bytes=62 * 1024 * 1024
        ),
    )(
        sheet, w_query.T, w_key.T, w_value.T,
        cotangent.transpose(0, 2, 1).reshape(16, NH, HEAD_DIM, 256), lengths,
    )
    out, wg = pl.pallas_call(
        place,
        out_shape=(jax.ShapeDtypeStruct(out.shape, BF16), jax.ShapeDtypeStruct(wg.shape, F32)),
        in_specs=[anyw, anyw],
        out_specs=(anyw, anyw),
        scratch_shapes=[V(out.shape, BF16), V(wg.shape, F32), dma((5,)), dma((5,))],
    )(out, wg)
    return out.transpose(0, 2, 1), wg


def solution(mesh):
    in_specs = (
        P("rows", None, None),
        P(None, "heads"),
        P(None, "heads"),
        P(None, "heads"),
        P("rows", None, "heads"),
        P("rows"),
    )
    out_specs = (P("rows", None, "heads"), P("rows", None, "heads"))
    return jax.shard_map(body, mesh=mesh, in_specs=in_specs, out_specs=out_specs, check_vma=False)
```

```python
import functools

import jax
import jax.numpy as jnp
from jax import lax
from jax.experimental import pallas as pl
from jax.experimental.pallas import tpu as pltpu
from jax.sharding import PartitionSpec as P

HEAD_DIM = 64
MESH = pl.DeviceIdType.MESH
NX, NZ, NY = 4, 8, 4
NH = 3
F32 = jnp.float32
BF16 = jnp.bfloat16


def nt(a, b):
    return lax.dot_general(a, b, (((1,), (1,)), ((), ())), preferred_element_type=F32)


def nn(a, b):
    return lax.dot_general(a, b, (((1,), (0,)), ((), ())), preferred_element_type=F32)


def tn(a, b):
    return lax.dot_general(a, b, (((0,), (0,)), ((), ())), preferred_element_type=F32)


def kernel(
    scale,
    sheet_h, wq, wk, wv, cot_h, lens, out_h, wg_out,
    sheet, w_t, w_c, w_vc, vm, q_t, k_t, v_t, g_t,
    w_far, wv_far, w_out, q_far, k_far, g_far,
    u, a_recv, a_sum, x_recv, x_sum, z_recv, full, gat, gat_far, prob, dsc,
    acc, out_v, wg_acc, wg_n, wg_b, wa_recv, wz_recv, wx_f, wx_sum, wx_recv,
    s_sheet, s_cot, s_w, s_out,
    sa, ra, sx, rx, sz, rz, sd, rd, sgz, rgz, sgx, rgx, sgc, rgc,
    swy, rwy, sww, rww, swc, rwc, sg, rg, sgr, rgr, sty, rty, soz, roz, sox, rox, soc, roc,
    swa, rwa, swx, rwx, swz, rwz,
):
    ri = lax.axis_index("rows")
    y = lax.axis_index("heads")
    core = lax.rem(ri, 2)
    x = lax.rem(ri // 2, NX)
    z = ri // (2 * NX)
    other = 1 - core
    block = x * NZ + z
    partner = {"rows": (z * NX + x) * 2 + other}
    xs = [lax.rem(x + k, NX) for k in range(1, NX)]
    zs = [lax.rem(z + k, NZ) for k in range(1, NZ)]
    ys = [lax.rem(y + k, NY) for k in range(1, NY)]
    xpeer = [{"rows": (z * NX + xk) * 2 + core} for xk in xs]
    zpeer = [{"rows": (zk * NX + x) * 2 + core} for zk in zs]
    ypeer = [{"heads": yk} for yk in ys]
    d_up, d_dn = ypeer[0], ypeer[2]

    def remote(src, dst, ss, rs, dev):
        return pltpu.make_async_remote_copy(
            src_ref=src, dst_ref=dst, send_sem=ss, recv_sem=rs, device_id=dev, device_id_type=MESH
        )

    sends = []

    def send(copies):
        for c in copies:
            c.start()

    def sent(ref, sem):
        sends.append((ref, sem))

    def flush():
        for ref, sem in sends:
            remote(ref, ref, sem, sem, partner).wait_send()

    def arrived(ref, sem):
        remote(ref, ref, sem, sem, partner).wait_recv()

    def w_copy(t):
        return pltpu.make_async_copy((wq, wk, wv)[t], w_t.at[192 * t:192 * t + 192], s_w.at[0])

    def sheet_copy(i):
        rows = pl.ds(4 * i, 4)
        return pltpu.make_async_copy(sheet_h.at[rows], sheet.at[rows], s_sheet.at[i])

    def cot_copy(r):
        return pltpu.make_async_copy(cot_h.at[r], g_t.at[:, 64 * r:64 * r + 64, :], s_cot.at[0])

    for t in range(3):
        w_copy(t).start()
    sheet_copy(0).start()

    barrier = pltpu.get_barrier_semaphore()
    peers = [partner] + ypeer + xpeer + zpeer
    for dev in peers:
        pl.semaphore_signal(barrier, inc=1, device_id=dev, device_id_type=MESH)

    for r in range(16):
        vm[r:r + 1, :] = (lax.broadcasted_iota(jnp.int32, (1, 256), 1) < lens[r]).astype(F32)

    def split_rows(ref, r, mat):
        at = pl.multiple_of(r * 64, 64)
        for h in range(NH):
            ref[h, pl.ds(at, 64), :] = mat[h * 64:(h + 1) * 64].astype(BF16)

    def value_rows(i, _):
        sheet_copy(i).wait()
        mat = nt(w_t[384:576], sheet[pl.ds(4 * i, 4)].reshape(1024, 768))
        for n in range(4):
            split_rows(v_t, 4 * i + n, mat[:, 256 * n:256 * n + 256] * vm[pl.ds(4 * i + n, 1), :])
        return 0

    pltpu.make_async_copy(w_t, w_t, s_w.at[0]).wait()
    for i in range(1, 4):
        sheet_copy(i).start()
    for r in range(16):
        cot_copy(r).start()
    w_vc[...] = w_t[384:576].T
    lax.fori_loop(0, 2, value_rows, 0)
    pl.semaphore_wait(barrier, len(peers))

    quarter = lax.rem(z, 4)
    piece = [quarter, x, x]

    def wy_copies():
        got = []
        for k in range(NY - 1):
            p = piece[k]
            src = w_t.at[pl.ds(pl.multiple_of(core * 192 + p * 48, 16), 48), :]
            got.append(remote(src, w_far.at[k, core, p], swy.at[0], rwy.at[0], ypeer[k]))
            src = w_vc.at[pl.ds(pl.multiple_of(ys[k] * 192 + p * 48, 16), 48), :]
            got.append(remote(src, wv_far.at[k, p], swy.at[1], rwy.at[1], ypeer[k]))
        return got

    hop2 = lax.rem(z + 2 + 4 * lax.rem(z, 2), NZ)
    wpeer = [zpeer[0], zpeer[NZ - 2], {"rows": (hop2 * NX + x) * 2 + core}]

    def wz_copies():
        got = []
        for k in range(3):
            ref = w_far.at[0, core, quarter]
            got.append(remote(ref, ref, sww.at[0], rww.at[0], wpeer[k]))
            ref = wv_far.at[0, quarter]
            got.append(remote(ref, ref, sww.at[1], rww.at[1], wpeer[k]))
        return got

    def wx_copies():
        got = []
        for k in range(3):
            ref = w_far.at[1:3, core, x]
            got.append(remote(ref, ref, sww.at[2], rww.at[2], xpeer[k]))
            ref = wv_far.at[1:3, x]
            got.append(remote(ref, ref, sww.at[3], rww.at[3], xpeer[k]))
        return got

    def near_copies(c):
        src = g_t.at[:, 128 * c:128 * c + 128, :]
        return [
            remote(src, g_far.at[0, :, 128 * c:128 * c + 128, :], sg.at[0], rg.at[0, c], d_up),
            remote(src, g_far.at[2, :, 128 * c:128 * c + 128, :], sg.at[1], rg.at[1, c], d_dn),
        ]

    def relay_copies(c):
        lo, hi = 128 * c, 128 * c + 64
        return [
            remote(
                g_far.at[0, :, lo:lo + 64, :], g_far.at[1, :, lo:lo + 64, :], sgr.at[0], rgr.at[c // 2], d_up
            ),
            remote(
                g_far.at[2, :, hi:hi + 64, :], g_far.at[1, :, hi:hi + 64, :], sgr.at[1], rgr.at[c // 2], d_dn
            ),
        ]

    def near(chunks):
        for c in chunks:
            for cp in near_copies(c):
                cp.start()

    def relay(chunks):
        for c in chunks:
            for got, cp in zip(near_copies(c), relay_copies(c)):
                got.wait_recv()
                cp.start()

    def core_copy(t, h):
        return remote(
            u.at[t, other, h], a_recv.at[t, h], sa.at[t], ra.at[t], partner
        )

    def x_copy(t, k):
        at = pl.multiple_of(xs[k] * 64, 64)
        return remote(
            a_sum.at[t, :, pl.ds(at, 64), :], x_recv.at[t, k], sx.at[t], rx.at[t], xpeer[k]
        )

    def z_copy(t, k):
        at = pl.multiple_of(zs[k] * 8, 8)
        return remote(
            x_sum.at[t, :, pl.ds(at, 8), :], z_recv.at[t, k], sz.at[t], rz.at[t], zpeer[k]
        )

    def outer(t, left, right):
        def one(h, _):
            mat = tn(left[h], right[h])
            u[t, 0, h] = mat[:, :128]
            u[t, 1, h] = mat[:, 128:]
            core_copy(t, h).start()
            return 0

        lax.fori_loop(0, NH, one, 0)
        sent(a_recv.at[t], sa.at[t])

    def add_core(t):
        arrived(a_recv.at[t], ra.at[t])
        a_sum[t] = u[t, core] + a_recv[t]
        send([x_copy(t, k) for k in range(NX - 1)])
        sent(x_recv.at[t], sx.at[t])

    def add_x(t):
        arrived(x_recv.at[t], rx.at[t])
        mine = pl.multiple_of(x * 64, 64)
        x_sum[t] = a_sum[t, :, pl.ds(mine, 64), :] + x_recv[t, 0] + x_recv[t, 1] + x_recv[t, 2]
        send([z_copy(t, k) for k in range(NZ - 1)])
        sent(z_recv.at[t], sz.at[t])

    def add_z(t):
        arrived(z_recv.at[t], rz.at[t])
        mine = pl.multiple_of(z * 8, 8)
        total = x_sum[t, :, pl.ds(mine, 8), :]
        for k in range(NZ - 1):
            total = total + z_recv[t, k]
        full[core, t] = total

    def query_rows(qr, kr, weights, lo, hi):
        def one(i, _):
            mat = nt(weights(), sheet[pl.ds(4 * i, 4)].reshape(1024, 768))
            for n in range(4):
                sub = mat[:, 256 * n:256 * n + 256] * vm[pl.ds(4 * i + n, 1), :]
                split_rows(qr, 4 * i + n, sub[:192])
                split_rows(kr, 4 * i + n, sub[192:])
            return 0

        lax.fori_loop(lo, hi, one, 0)

    def own_weights():
        return w_t[0:384]

    def far_weights(s):
        w_c[...] = w_far[s].reshape(384, 768).T
        w_out[s + 1, :, 0:384] = w_c[rows_y, :]
        w_out[s + 1, :, 384:576] = wv_far[s].reshape(192, 192)

    def far_rows(s, lo, hi):
        if lo == 0:
            far_weights(s)
        query_rows(q_far.at[s], k_far.at[s], lambda: w_far[s].reshape(384, 768), lo, hi)

    send(wy_copies())
    sent(w_far.at[:, 0, 0], swy.at[0])
    sent(wv_far.at[:, 0], swy.at[1])
    lax.fori_loop(2, 4, value_rows, 0)
    pltpu.make_async_copy(g_t, g_t, s_cot.at[0]).wait()
    outer(0, g_t, v_t)
    query_rows(q_t, k_t, own_weights, 0, 1)
    add_core(0)
    query_rows(q_t, k_t, own_weights, 1, 4)
    outer(1, q_t, k_t)
    arrived(w_far.at[:, 0, 0], rwy.at[0])
    arrived(wv_far.at[:, 0], rwy.at[1])
    send(wz_copies())
    near([0, 1, 2])
    add_core(1)
    send(wx_copies())
    sent(w_far.at[:, 0, 0], sww.at[0])
    sent(wv_far.at[:, 0], sww.at[1])
    sent(w_far.at[:, :, 0], sww.at[2])
    sent(wv_far.at[:, 0:2], sww.at[3])
    add_x(0)
    rows_y = pl.ds(pl.multiple_of(y * 192, 16), 192)
    w_c[...] = w_t[0:384].T
    w_out[0, :, 0:384] = w_c[rows_y, :]
    w_out[0, :, 384:576] = w_vc[rows_y, :]
    add_x(1)
    relay([0])
    arrived(w_far.at[:, 0, 0], rww.at[0])
    arrived(wv_far.at[:, 0], rww.at[1])
    wc_copy = remote(w_far.at[0, core], w_far.at[0, core], swc.at[0], rwc.at[0], partner)
    wd_copy = remote(w_far.at[1:3, core], w_far.at[1:3, core], swc.at[1], rwc.at[1], partner)
    send([wc_copy])
    sent(w_far.at[0, 0], swc.at[0])
    wc_copy.wait_recv()
    far_rows(0, 0, 4)
    relay([1])
    add_z(0)
    add_z(1)

    half_copy = remote(full.at[core], full.at[core], sd.at[0], rd.at[0], partner)
    send([half_copy])
    sent(full.at[0], sd.at[0])
    half_copy.wait_recv()

    dprob = jnp.concatenate([full[0, 0], full[1, 0]], axis=-1)
    logits = jnp.concatenate([full[0, 1], full[1, 1]], axis=-1) * scale
    top = jnp.max(logits, axis=-1, keepdims=True)
    ex = jnp.exp(logits - top)
    probs = ex / jnp.sum(ex, axis=-1, keepdims=True)
    inner = jnp.sum(probs * dprob, axis=-1, keepdims=True)
    dscore = scale * probs * (dprob - inner)
    tile = jnp.concatenate([probs, dscore], axis=1)
    gat[core, block] = jnp.where(core == 0, tile[:, :, :128], tile[:, :, 128:]).astype(BF16)

    own = gat.at[core, block]
    gz = [remote(own, own, sgz.at[0], rgz.at[0], zpeer[k]) for k in range(NZ - 1)]
    ty = [
        remote(own, gat_far.at[k, core, block], sty.at[0], rty.at[0], ypeer[k]) for k in range(NY - 1)
    ]
    send(gz)
    send(ty)
    sent(gat.at[0, 0:7], sgz.at[0])
    sent(gat_far.at[:, 0, 0], sty.at[0])
    near([3, 4, 5, 6, 7])

    xblock = pl.ds(pl.multiple_of(x * NZ, NZ), NZ)

    def gx_copy(k):
        src = gat.at[core, xblock]
        return remote(src, src, sgx.at[0], rgx.at[k], xpeer[k])

    def from_x(k):
        return pl.ds(pl.multiple_of(lax.rem(x + NX - k, NX) * NZ, NZ), NZ)

    def gc_copy(k):
        src = gat.at[core, from_x(k)]
        return remote(src, src, sgc.at[0], rgc.at[0], partner)

    def oz_copy(k):
        src = gat_far.at[:, core, block]
        return remote(src, src, soz.at[0], roz.at[0], zpeer[k])

    def ox_copy(s, k):
        src = gat_far.at[s, core, xblock]
        return remote(src, src, sox.at[0], rox.at[s], xpeer[k])

    def oc_copy(s, k):
        src = gat_far.at[s, core, from_x(k)]
        return remote(src, src, soc.at[0], roc.at[s], partner)

    arrived(w_far.at[:, :, 0], rww.at[2])
    arrived(wv_far.at[:, 0:2], rww.at[3])
    send([wd_copy])
    sent(w_far.at[1:3, 0], swc.at[1])
    wd_copy.wait_recv()
    far_rows(1, 0, 2)
    arrived(gat.at[0, 0:7], rgz.at[0])
    send([gx_copy(k) for k in range(NX - 1)])
    send([gc_copy(0)])
    arrived(gat_far.at[:, 0, 0], rty.at[0])
    send([oz_copy(k) for k in range(NZ - 1)])
    far_rows(1, 2, 4)
    far_rows(2, 0, 4)
    relay([2])
    for k in range(NX - 1):
        gx_copy(k).wait_recv()
        send([gc_copy(k + 1)])
    sent(gat.at[0, 0:24], sgx.at[0])
    sent(gat.at[0], sgc.at[0])
    arrived(gat.at[0], rgc.at[0])

    def unpack(src):
        def one(h, _):
            for ch in range(2):
                mat = src(ch, h).astype(F32)
                prob[h, :, ch * 128:(ch + 1) * 128] = mat[:, :8].reshape(256, 128).astype(BF16)
                dsc[h, :, ch * 128:(ch + 1) * 128] = mat[:, 8:].reshape(256, 128).astype(BF16)
            return 0

        lax.fori_loop(0, NH, one, 0)

    def masked(ref, h, mat):
        for r in range(16):
            ref[h, r * 64:(r + 1) * 64, :] = (mat[r * 64:(r + 1) * 64] * vm[r:r + 1, :]).astype(BF16)

    def back_qk(qr, kr):
        def one(h, _):
            dq = nt(kr[h], dsc[h])
            dk = nn(qr[h], dsc[h])
            masked(qr, h, dq)
            masked(kr, h, dk)
            return 0

        lax.fori_loop(0, NH, one, 0)

    def gathered(refs, c):
        cols = []
        for n in range(4):
            at = pl.multiple_of(c * 256 + n * 64, 64)
            cols.append(jnp.concatenate([ref[h, pl.ds(at, 64), :] for ref in refs for h in range(NH)], axis=0))
        return jnp.concatenate(cols, axis=1)

    unpack(lambda ch, h: gat[ch, :, h])
    back_qk(q_t, k_t)

    def back_v(h, _):
        masked(v_t, h, nn(g_t[h], prob[h]))
        return 0

    lax.fori_loop(0, NH, back_v, 0)
    relay([3])
    wg_acc[...] = jnp.zeros_like(wg_acc)

    def own_wg(c, _):
        wg_acc[...] += nn(gathered((q_t, k_t, v_t), c), sheet[pl.ds(4 * c, 4)].reshape(1024, 768))
        return 0

    def own_out(c, _):
        acc[c] = nn(w_out[0], gathered((q_t, k_t, v_t), c))
        return 0

    lax.fori_loop(0, 1, own_wg, 0)
    arrived(gat_far.at[:, 0, 0:7], roz.at[0])
    sent(gat_far.at[:, 0, 0:7], soz.at[0])
    send([ox_copy(s, k) for s in (0, 2, 1) for k in range(NX - 1)])
    send([oc_copy(s, 0) for s in range(NY - 1)])
    sent(gat_far.at[:, 0, 0:24], sox.at[0])
    sent(gat_far.at[:, 0], soc.at[0])
    lax.fori_loop(1, 4, own_wg, 0)
    wg_n[...] = wg_acc[...].T
    for gc in range(2):
        for gz_ in range(NZ):
            rows = [wg_n[12 * g:12 * g + 12, :] for g in range(8 * gz_ + gc, 8 * gz_ + 8, 2)]
            wg_b[gc, gz_] = jnp.concatenate(rows, axis=0).astype(BF16)
    wa = remote(wg_b.at[other], wa_recv, swa.at[0], rwa.at[0], partner)
    send([wa])
    sent(wa_recv, swa.at[0])
    relay([4, 5])
    lax.fori_loop(0, 4, own_out, 0)

    def far_ready(s):
        arrived(gat_far.at[s, 0, 0:24], rox.at[s])
        send([oc_copy(s, k + 1) for k in range(NX - 1)])

    def wz_copy(k):
        return remote(wa_recv.at[zs[k]], wz_recv.at[k], swz.at[0], rwz.at[0], zpeer[k])

    def wx_copy(k):
        return remote(wx_sum.at[xs[k]], wx_recv.at[k], swx.at[0], rwx.at[0], xpeer[k])

    def far_qk(s):
        arrived(gat_far.at[s, 0], roc.at[s])
        unpack(lambda ch, h: gat_far[s, ch, :, h])
        back_qk(q_far.at[s], k_far.at[s])

    def far_v(s, h, c):
        at = pl.multiple_of(c * 256, 256)
        mat = nn(g_far[s, h, pl.ds(at, 256), :], prob[h])
        return [
            (mat[n * 64:(n + 1) * 64] * vm[pl.ds(4 * c + n, 1), :]).astype(BF16) for n in range(4)
        ]

    def far_v_mat(s, c):
        parts = [far_v(s, h, c) for h in range(NH)]
        return jnp.concatenate(
            [jnp.concatenate([parts[h][n] for h in range(NH)], axis=0) for n in range(4)], axis=1
        )

    def far_out(s, lo, hi):
        def one(c, _):
            grads = jnp.concatenate([gathered((q_far.at[s], k_far.at[s]), c), far_v_mat(s, c)], axis=0)
            acc[c] += nn(w_out[s + 1], grads)
            return 0

        lax.fori_loop(lo, hi, one, 0)

    wa.wait_recv()
    wa_recv[...] = (wa_recv[...].astype(F32) + wg_b[core].astype(F32)).astype(BF16)
    send([wz_copy(k) for k in range(NZ - 1)])
    sent(wz_recv, swz.at[0])
    far_ready(0)
    far_qk(0)
    relay([6, 7])
    far_out(0, 0, 2)
    far_ready(2)
    far_out(0, 2, 4)
    far_qk(2)
    far_out(2, 0, 3)
    far_ready(1)
    far_out(2, 3, 4)
    far_qk(1)
    arrived(wz_recv, rwz.at[0])
    wsum = wa_recv[z].astype(F32)
    for k in range(NZ - 1):
        wsum = wsum + wz_recv[k].astype(F32)
    wx_f[0:48] = wsum
    wx_f[48:56] = jnp.zeros((8, 576), F32)
    for n in range(NX):
        wx_sum[n] = wx_f[12 * n:12 * n + 16, :].astype(BF16)
    send([wx_copy(k) for k in range(NX - 1)])
    sent(wx_recv, swx.at[0])


    def out_copy(c):
        rows = pl.ds(4 * c, 4)
        return pltpu.make_async_copy(out_v.at[rows], out_h.at[rows], s_out.at[0])

    for c in range(4):
        arrived(g_far.at[1, :, 256 * c:256 * c + 256, :], rgr.at[c])
        grads = jnp.concatenate([gathered((q_far.at[1], k_far.at[1]), c), far_v_mat(1, c)], axis=0)
        tot = acc[c] + nn(w_out[2], grads)
        for n in range(4):
            out_v[4 * c + n] = tot[:, 256 * n:256 * n + 256].astype(BF16)
        out_copy(c).start()

    arrived(wx_recv, rwx.at[0])
    total = wx_sum[x].astype(F32)
    for k in range(NX - 1):
        total = total + wx_recv[k].astype(F32)
    for t in range(3):
        wg_out[:, t, :] = total[:12, 192 * t:192 * t + 192]

    for n in range(2):
        sent(g_t, sg.at[n])
        sent(g_far.at[1, :, 0:512, :], sgr.at[n])
    flush()
    pltpu.make_async_copy(out_v, out_v, s_out.at[0]).wait()


def place(out_h, wg_h, out_f, wg_f, out_v, wg_v, s_in, s_out):
    def pieces(src, dst, sem):
        got = [pltpu.make_async_copy(src[1], dst[1], sem.at[4])]
        for c in range(4):
            rows = pl.ds(4 * c, 4)
            got.append(pltpu.make_async_copy(src[0].at[rows], dst[0].at[rows], sem.at[c]))
        return got

    first = pieces((out_h, wg_h), (out_v, wg_v), s_in)
    second = pieces((out_v, wg_v), (out_f, wg_f), s_out)
    for c in first:
        c.start()
    for a, b in zip(first, second):
        a.wait()
        b.start()
    for c in second:
        c.wait()


def body(sheet, w_query, w_key, w_value, cotangent, lengths):
    scale = float((HEAD_DIM * sheet.shape[0] * lax.axis_size("rows")) ** -0.5)
    vmem = pl.BlockSpec(memory_space=pltpu.VMEM)
    anyw = pl.BlockSpec(memory_space=pl.ANY)
    dma = pltpu.SemaphoreType.DMA
    V = pltpu.VMEM
    rows = (3, 1024, 256)
    scratch = [
        V((16, 256, 768), BF16), V((576, 768), BF16), V((768, 384), BF16), V((768, 192), BF16), V((16, 256), F32),
        V(rows, BF16), V(rows, BF16), V(rows, BF16), V(rows, BF16),
        V((3, 2, 4, 48, 768), BF16), V((3, 4, 48, 192), BF16), V((4, 192, 576), BF16),
        V((3,) + rows, BF16), V((3,) + rows, BF16), V((3,) + rows, BF16),
        V((2, 2, 3, 256, 128), F32), V((2, 3, 256, 128), F32), V((2, 3, 256, 128), F32),
        V((2, 3, 3, 64, 128), F32), V((2, 3, 64, 128), F32),
        V((2, 7, 3, 8, 128), F32), V((2, 2, 3, 8, 128), F32),
        V((2, 32, 3, 16, 128), BF16), V((3, 2, 32, 3, 16, 128), BF16),
        V((3, 256, 256), BF16), V((3, 256, 256), BF16),
        V((4, 192, 1024), F32), V((16, 192, 256), BF16),
        V((576, 768), F32), V((768, 576), F32), V((2, 8, 48, 576), BF16), V((8, 48, 576), BF16),
        V((7, 48, 576), BF16), V((56, 576), F32), V((4, 16, 576), BF16), V((3, 16, 576), BF16),
        dma((4,)), dma((1,)), dma((1,)), dma((1,)),
    ]
    shapes = [
        (2, 2), (2, 2), (2, 2), (1, 1), (1, 1), (1, 3), (1, 1),
        (2, 2), (4, 4), (2, 2), (2, (2, 8)), (2, 4), (1, 1), (1, 1), (1, 3), (1, 3),
        (1, 1), (1, 1), (1, 1),
    ]
    for out_shape, in_shape in shapes:
        scratch += [dma(shape if isinstance(shape, tuple) else (shape,)) for shape in (out_shape, in_shape)]
    out, wg = pl.pallas_call(
        functools.partial(kernel, scale),
        out_shape=(jax.ShapeDtypeStruct((16, 192, 256), BF16), jax.ShapeDtypeStruct((12, 3, 192), F32)),
        in_specs=[anyw] * 5 + [pl.BlockSpec(memory_space=pltpu.SMEM)],
        out_specs=(anyw, vmem),
        scratch_shapes=scratch,
        compiler_params=pltpu.CompilerParams(
            collective_id=0, has_side_effects=True, vmem_limit_bytes=62 * 1024 * 1024
        ),
    )(
        sheet, w_query.T, w_key.T, w_value.T,
        cotangent.transpose(0, 2, 1).reshape(16, NH, HEAD_DIM, 256), lengths,
    )
    out, wg = pl.pallas_call(
        place,
        out_shape=(jax.ShapeDtypeStruct(out.shape, BF16), jax.ShapeDtypeStruct(wg.shape, F32)),
        in_specs=[anyw, anyw],
        out_specs=(anyw, anyw),
        scratch_shapes=[V(out.shape, BF16), V(wg.shape, F32), dma((5,)), dma((5,))],
    )(out, wg)
    return out.transpose(0, 2, 1), wg


def solution(mesh):
    in_specs = (
        P("rows", None, None),
        P(None, "heads"),
        P(None, "heads"),
        P(None, "heads"),
        P("rows", None, "heads"),
        P("rows"),
    )
    out_specs = (P("rows", None, "heads"), P("rows", None, "heads"))
    return jax.shard_map(body, mesh=mesh, in_specs=in_specs, out_specs=out_specs, check_vma=False)
```
